32 devices in a mesh: sect: 4 (over y, x), dev: 8 (over z, core).
Axes of the slice: x: 2, y: 2, z: 4, core: 2. Of those that a mesh axis runs over, the one named last changes fastest.
Arguments:
- voltages: bfloat16 [2, 2048, 65536], P(None, 'sect', 'dev'), may hold values from -6 to 6
- filter_taps: float32 [4, 1024], replicated, may hold values from -3 to 3
- feed_tile: int32 [2048], P('sect'), may hold values from 0 to 127
- bad_feed: int32 [2048], P('sect'), may hold values 0 or 1
- delays: float32 [1024, 128], P('sect'), may hold values from -32 to 32
Outputs:
- visibilities: float32 [2, 1024, 128, 128], P(None, 'dev', 'sect')
- beams: bfloat16 [2, 1024, 1024, 64], P(None, 'dev', 'sect')
The draws below stay inside these ranges and needn't reach their ends.
Inputs may be any that keep to these rules, and one draw needn't show every extreme that they name: `feed_tile`: each feed belongs to one tile.
All inputs are finite; a program needn't handle non-finite values. No bound on the sum of `bad_feed` on one device may be relied on, other than what follows from the above.
Results may differ from the reference program's by a relative error of at most 0.014.
Values may be sent and summed in bfloat16 or wider, within the bound.
A program may use at most 192 MiB of HBM per device.

```python
import math
import jax
import jax.numpy as jnp
from jax import lax

FEEDS = 2048
CHANNELS = 1024
TILES = 128
BEAMS = 1024
TAPS = 4
FRAMES = 64
SAMPLES = 65536
N_SECT = 4


def place_ends(entries, rng, low, top_value):
    extent = entries.shape
    index_at = [jax.random.randint(jax.random.fold_in(rng, axis), (), 0, extent[axis]) for axis in range(len(extent))]
    entries = entries.at[tuple(index_at)].set(low)
    longest = extent.index(max(extent))
    index_at[longest] = (index_at[longest] + 1) % extent[longest]
    return entries.at[tuple(index_at)].set(top_value)


def steps_of(key, dims, shards, low, largest):
    factor_of = 1.0
    for dim, parts in shards:
        draws = jax.random.uniform(jax.random.fold_in(jax.random.fold_in(key, 6), dim), (parts,), jnp.float32, low / len(shards), largest / len(shards))
        factor_of = factor_of * jnp.repeat(jnp.exp(draws), dims[dim] // parts).reshape((-1,) + (1,) * (len(dims) - 1 - dim))
    return factor_of


def bell_draw(key, dims, scale, bound, shards=(), kind=jnp.bfloat16):
    gain = steps_of(key, dims, shards, -0.22, 0.18) if shards else 1.0
    drawn = jax.random.normal(key, dims, jnp.float32) * scale * gain
    return jnp.minimum(jnp.maximum(drawn, -bound), bound).astype(kind)


def setup_inputs(seed: int = 0) -> dict:
    key_list = jax.random.split(jax.random.key(seed), 6)
    voltages = bell_draw(key_list[0], (2, FEEDS, SAMPLES), 1.0, 6.0, ((1, 4), (2, 8)))
    filter_taps = bell_draw(key_list[1], (TAPS, CHANNELS), 0.5, 3.0, (), jnp.float32)
    feed_tile = place_ends(jax.random.randint(key_list[2], (FEEDS,), 0, TILES), jax.random.fold_in(key_list[2], 1), 0, TILES - 1).astype(jnp.int32)
    bad_feed = place_ends((jax.random.randint(key_list[3], (FEEDS,), 0, 8) < 1).astype(jnp.int32), jax.random.fold_in(key_list[3], 1), 0, 1)
    delays = jnp.clip(jax.random.uniform(key_list[4], (BEAMS, TILES), jnp.float32, -32.0, 32.0) * steps_of(key_list[4], (BEAMS, TILES), ((0, 4),), -0.4, 0.0), -32.0, 32.0)
    return {"voltages": voltages, "filter_taps": filter_taps, "feed_tile": feed_tile, "bad_feed": bad_feed, "delays": delays}


def fourier_tables():
    positions = jnp.arange(CHANNELS, dtype=jnp.int32)
    product = positions[:, None] * positions[None, :] % CHANNELS
    phase_angle = product.astype(jnp.float32) * (2.0 * math.pi / CHANNELS)
    factor = 1.0 / math.sqrt(CHANNELS)
    cosine_table = (jnp.cos(phase_angle) * factor).astype(jnp.bfloat16)
    sine_table = (jnp.sin(phase_angle) * factor).astype(jnp.bfloat16)
    return (cosine_table, sine_table)

def filter_bank(window, filter_taps, frames):
    running = jnp.zeros((2, window.shape[1], frames, window.shape[3]), jnp.float32)
    for tap_index in range(TAPS):
        begin_frame = TAPS - 1 - tap_index
        running = running + filter_taps[tap_index] * window[:, :, begin_frame:begin_frame + frames].astype(jnp.float32)
    return running.astype(jnp.bfloat16)

def transform(filtered, cosine_table, sine_table):
    real_part = jnp.dot(filtered[0], cosine_table, preferred_element_type=jnp.float32) + jnp.dot(filtered[1], sine_table, preferred_element_type=jnp.float32)
    quad_part = jnp.dot(filtered[1], cosine_table, preferred_element_type=jnp.float32) - jnp.dot(filtered[0], sine_table, preferred_element_type=jnp.float32)
    return jnp.stack([real_part, quad_part]).astype(jnp.bfloat16)

def tile_matrix(feed_tile, bad_feed):
    tile_ids = jnp.arange(TILES, dtype=jnp.int32)
    member = (feed_tile[:, None] == tile_ids[None, :]) & (bad_feed[:, None] == 0)
    return jnp.where(member, 1.0, 0.0).astype(jnp.bfloat16)

def reference(voltages, filter_taps, feed_tile, bad_feed, delays):
    cosine_table, sine_table = fourier_tables()
    block_feeds = FEEDS // N_SECT

    def add_section(section, running):
        first_feed = (section * block_feeds).astype(jnp.int32)
        block = lax.dynamic_slice_in_dim(voltages, first_feed, block_feeds, 1)
        block = block.reshape(2, block_feeds, FRAMES, CHANNELS)
        window = jnp.pad(block, ((0, 0), (0, 0), (TAPS - 1, 0), (0, 0)))
        spectra = transform(filter_bank(window, filter_taps, FRAMES), cosine_table, sine_table)
        matrix = tile_matrix(lax.dynamic_slice_in_dim(feed_tile, first_feed, block_feeds, 0), lax.dynamic_slice_in_dim(bad_feed, first_feed, block_feeds, 0))
        partial_value = jnp.einsum('zfnc,fa->zanc', spectra.astype(jnp.float32), matrix.astype(jnp.float32))
        rounded = lax.optimization_barrier(partial_value.astype(jnp.bfloat16))
        return running + rounded.astype(jnp.float32)
    initial = jnp.zeros((2, TILES, FRAMES, CHANNELS), jnp.float32)
    running = lax.fori_loop(0, N_SECT, add_section, initial)
    tile_volts = running.astype(jnp.bfloat16)
    volts_real = tile_volts[0].astype(jnp.float32)
    volts_quad = tile_volts[1].astype(jnp.float32)
    vis_scale = 1.0 / (FRAMES * FEEDS / TILES)
    real_part = jnp.einsum('atc,btc->cab', volts_real, volts_real) + jnp.einsum('atc,btc->cab', volts_quad, volts_quad)
    quad_part = jnp.einsum('atc,btc->cab', volts_quad, volts_real) - jnp.einsum('atc,btc->cab', volts_real, volts_quad)
    visibilities = jnp.stack([real_part, quad_part]) * vis_scale
    channel = jnp.arange(CHANNELS, dtype=jnp.int32).astype(jnp.float32)
    block_beams = BEAMS // N_SECT

    def beam_block(section):
        delay_rows = lax.dynamic_slice_in_dim(delays, (section * block_beams).astype(jnp.int32), block_beams, 0)
        phase_angle = delay_rows[None, :, :] * channel[:, None, None] * (2.0 * math.pi / CHANNELS)
        weight_cos = jnp.cos(phase_angle).astype(jnp.bfloat16).astype(jnp.float32)
        weight_sin = jnp.sin(phase_angle).astype(jnp.bfloat16).astype(jnp.float32)
        beam_real = jnp.einsum('cba,atc->cbt', weight_cos, volts_real) + jnp.einsum('cba,atc->cbt', weight_sin, volts_quad)
        beam_quad = jnp.einsum('cba,atc->cbt', weight_cos, volts_quad) - jnp.einsum('cba,atc->cbt', weight_sin, volts_real)
        return jnp.stack([beam_real, beam_quad])
    stacked = lax.map(beam_block, jnp.arange(N_SECT, dtype=jnp.int32))
    beams = jnp.transpose(stacked, (1, 2, 0, 3, 4)).reshape(2, CHANNELS, BEAMS, FRAMES)
    beams = (beams * (1.0 / math.sqrt(FEEDS))).astype(jnp.bfloat16)
    return (visibilities, beams)
```

```python
import functools
import math

import jax
import jax.numpy as jnp
from jax import lax
from jax.experimental import pallas as pl
from jax.experimental.pallas import tpu as pltpu
from jax.sharding import PartitionSpec as P

FEEDS = 2048
TILES = 128
TAPS = 4
LOW = 8
QUARTERS = 4
LAG = 2

MESH = pl.DeviceIdType.MESH
BF16 = jnp.bfloat16
F32 = jnp.float32


def turn_trig(turns):
    r = turns - jnp.round(turns)
    y = r * math.pi
    q = y * y
    s = 0.0
    for n in (11, 9, 7, 5, 3, 1):
        s = s * q + (-1.0) ** ((n - 1) // 2) / math.factorial(n)
    s = s * y
    c = 0.0
    for n in (12, 10, 8, 6, 4, 2, 0):
        c = c * q + (-1.0) ** (n // 2) / math.factorial(n)
    return 1.0 - 2.0 * s * s, 2.0 * s * c


def correlate_kernel(
    n_sect, n_dev, vis_scale, beam_scale,
    volts, taps_in, tile_in, bad_in, delays_in,
    vis, beams,
    big, taps, feed_tile, bad_feed, delays, matrix, sums, share, tables, stack, turned,
    blocks, full, gathered, hist_src, hist_land, l1x, l1y, l2x, l2y,
    in_sem, volt_sem, h_send, h_recv, s1x_send, s1x_recv, s1y_send, s1y_recv,
    s2x_send, s2x_recv, s2y_send, s2y_recv, a_send, a_recv,
    gx_send, gx_recv, gy_send, gy_recv, rx_send, rx_recv, ry_send, ry_recv,
):
    me_s, me_d = lax.axis_index("sect"), lax.axis_index("dev")
    rows = n_sect // 2
    side, row = lax.rem(me_s, 2), me_s // 2
    across = row * 2 + 1 - side
    channels = taps.shape[1]
    groups = volts.shape[1]
    frames = volts.shape[3] // channels
    phases = frames // n_sect
    width = big.shape[2]
    n_chunk = channels // width
    _, chans, times, n_beam = beams.shape
    pieces = TILES // times
    own = vis.shape[2]

    def at_row(i):
        return lax.rem(row + i, rows)

    small = [
        pltpu.make_async_copy(a, b, in_sem.at[i])
        for i, (a, b) in enumerate(
            [(tile_in, feed_tile), (bad_in, bad_feed), (taps_in, taps), (delays_in, delays)]
        )
    ]

    def load(j, z, f):
        slot = ((j * 2 + z) * frames + f) * groups
        start = pl.multiple_of(f * channels + j * width, width)
        return pltpu.make_async_copy(
            volts.at[z, :, :, pl.ds(start, width)], big.at[pl.ds(slot, groups)],
            volt_sem.at[j, z, f],
        )

    for copy in small:
        copy.start()

    @pl.loop(0, n_chunk)
    def _(j):
        for z in range(2):
            for f in range(frames):
                load(j, z, f).start()

    barrier = pltpu.get_barrier_semaphore()
    for o in range(1, n_dev):
        pl.semaphore_signal(
            barrier, inc=1, device_id=(me_s, lax.rem(me_d + o, n_dev)), device_id_type=MESH
        )
    pl.semaphore_signal(barrier, inc=1, device_id=(across, me_d), device_id_type=MESH)
    for i in range(1, rows):
        pl.semaphore_signal(
            barrier, inc=1, device_id=(at_row(i) * 2 + side, me_d), device_id_type=MESH
        )

    @pl.when(me_d == 0)
    def _():
        hist_land[...] = jnp.zeros_like(hist_land)

    for copy in small[:2]:
        copy.wait()
    tile_ids = lax.broadcasted_iota(jnp.int32, (TILES, matrix.shape[2]), 0)
    for g in range(groups):
        span = slice(g * matrix.shape[2], (g + 1) * matrix.shape[2])
        member = (feed_tile[:, span] == tile_ids) & (bad_feed[:, span] == 0)
        matrix[g] = jnp.where(member, 1.0, 0.0).astype(BF16)
    for copy in small[2:]:
        copy.wait()
    pl.semaphore_wait(barrier, n_dev - 1 + rows)

    def push(source, target, send, recv, device):
        return pltpu.make_async_remote_copy(
            src_ref=source, dst_ref=target, send_sem=send, recv_sem=recv,
            device_id=device, device_id_type=MESH,
        )

    def part_at(p, j, pos):
        return ((p * n_chunk + j) * n_sect + pos) * pieces

    def part(z, p, j, pos, count=1):
        return beams.at[z, pl.ds(part_at(p, j, pos), count * pieces)]

    def store_part(z, p, j, pos, value):
        begin = part_at(p, j, pos)
        for n in range(pieces):
            beams[z, begin + n] = value[n * times : (n + 1) * times]

    def s1x(p, j):
        return push(
            part(0, p, j, (1 - side) * rows, rows), l1x.at[p, j],
            s1x_send.at[p, j], s1x_recv.at[p, j], (across, me_d),
        )

    def s1y(p, j, i):
        other = at_row(i)
        return push(
            part(1, p, j, other * 2, 2), l1y.at[p, j, i - 1],
            s1y_send.at[p, j, i - 1], s1y_recv.at[p, j, i - 1], (other * 2 + side, me_d),
        )

    def s2x(p, j, i):
        other = at_row(i)
        return push(
            part(0, p, j, side * rows + other), l2x.at[p, j, i - 1],
            s2x_send.at[p, j, i - 1], s2x_recv.at[p, j, i - 1], (other * 2 + side, me_d),
        )

    def s2y(p, j):
        return push(
            part(1, p, j, row * 2 + 1 - side), l2y.at[p, j],
            s2y_send.at[p, j], s2y_recv.at[p, j], (across, me_d),
        )

    def start_first(p, j, z):
        if z == 0:
            s1x(p, j).start()
        else:
            for i in range(1, rows):
                s1y(p, j, i).start()

    def history(j, z):
        return push(
            hist_src.at[j, z], hist_land.at[j, z], h_send.at[j, z], h_recv.at[j, z],
            (me_s, lax.rem(me_d + 1, n_dev)),
        )

    def position(z, f):
        s = f % n_sect
        return (s % 2) * rows + s // 2 if z == 0 else s

    def tap(m, j):
        return taps[m : m + 1, pl.ds(pl.multiple_of(j * width, width), width)]

    def keep_at(j, z, f, h):
        slot = ((j * 2 + z) * (TAPS - 1) + f) * (width // TILES) + h
        return pl.ds(pl.multiple_of(slot * TILES, TILES), TILES)

    @pl.loop(0, n_chunk)
    def _(j):
        for z in range(2):
            for f in range(frames):
                load(j, z, f).wait()
                slot = ((j * 2 + z) * frames + f) * groups
                total = 0.0
                for g in range(groups):
                    total = total + jnp.dot(
                        matrix[g], big[slot + g], preferred_element_type=F32
                    )
                sums[f] = total
                late = f - (frames - TAPS + 1)
                if late >= 0:
                    hist_src[j, z, late] = total.astype(BF16)

            @pl.when(me_d < n_dev - 1)
            def _():
                history(j, z).start()

            for f in range(frames - 1, -1, -1):
                total = 0.0
                for m in range(min(f + 1, TAPS)):
                    total = total + tap(m, j) * sums[f - m]
                if f >= TAPS - 1:
                    store_part(z, f // n_sect, j, position(z, f), total.astype(BF16))
                else:
                    for h in range(width // TILES):
                        share[keep_at(j, z, f, h), :] = total[:, h * TILES : (h + 1) * TILES]
                if f >= n_sect and f % n_sect == 0:
                    start_first(f // n_sect, j, z)

    span = 32
    col = lax.broadcasted_iota(jnp.int32, (span, channels), 1).astype(F32)
    line = lax.broadcasted_iota(jnp.int32, (span, channels), 0).astype(F32)
    cb, sb = turn_trig(line * col * (1.0 / channels))
    factor = 1.0 / math.sqrt(channels)
    sums_flat = channels // width
    for n in range(sums_flat):
        cut = slice(n * width, (n + 1) * width)
        sums[n, :span, :] = cb[:, cut] * factor
        sums[n, span : 2 * span, :] = sb[:, cut] * factor
    one = lax.broadcasted_iota(jnp.int32, (8, width), 1).astype(F32)

    @pl.loop(0, channels // span)
    def _(k):
        for n in range(sums_flat):
            turns = (one + float(n * width)) * (k * span).astype(F32) * (1.0 / channels)
            ca, sa = turn_trig(turns)
            ca, sa = ca[:1], sa[:1]
            low_c, low_s = sums[n, :span, :], sums[n, span : 2 * span, :]
            at = pl.ds(pl.multiple_of(k * span, span), span)
            cut = slice(n * width, (n + 1) * width)
            tables[0, at, cut] = (ca * low_c - sa * low_s).astype(BF16)
            tables[1, at, cut] = (sa * low_c + ca * low_s).astype(BF16)

    def add(*terms):
        total = terms[0].astype(F32)
        for term in terms[1:]:
            total = total + term.astype(F32)
        return total.astype(BF16)

    def middle(p, j):
        s1x(p, j).wait_recv()
        for i in range(1, rows):
            other = at_row(i)
            begin = part_at(p, j, side * rows + other)
            for n in range(pieces):
                beams[0, begin + n] = add(beams[0, begin + n], l1x[p, j, other * pieces + n])
            s2x(p, j, i).start()
        for i in range(1, rows):
            s1y(p, j, i).wait_recv()
        begin = part_at(p, j, row * 2 + 1 - side)
        for n in range(pieces):
            beams[1, begin + n] = add(
                beams[1, begin + n],
                *[l1y[p, j, i - 1, (1 - side) * pieces + n] for i in range(1, rows)],
            )
        s2y(p, j).start()

    def finish(p, j):
        at = pl.ds(pl.multiple_of(j * width, width), width)
        for i in range(1, rows):
            s2x(p, j, i).wait_recv()
        begin = part_at(p, j, side * rows + row)
        for n in range(pieces):
            value = add(
                beams[0, begin + n], l1x[p, j, row * pieces + n],
                *[l2x[p, j, i - 1, n] for i in range(1, rows)],
            )
            stack[n * times : (n + 1) * times, at] = value
            turned[TILES + n * times : TILES + (n + 1) * times, at] = -value
        s2y(p, j).wait_recv()
        begin = part_at(p, j, row * 2 + side)
        for n in range(pieces):
            value = add(
                beams[1, begin + n], l2y[p, j, n],
                *[l1y[p, j, i - 1, side * pieces + n] for i in range(1, rows)],
            )
            stack[TILES + n * times : TILES + (n + 1) * times, at] = value
            turned[n * times : (n + 1) * times, at] = value

    def late_frames(j):
        for z in range(2):
            @pl.when(me_d > 0)
            def _():
                history(j, z).wait_recv()

            for f in range(TAPS - 1):
                total = jnp.concatenate(
                    [share[keep_at(j, z, f, h), :] for h in range(width // TILES)], axis=1
                )
                for m in range(f + 1, TAPS):
                    total = total + tap(m, j) * hist_land[j, z, f - m + TAPS - 1].astype(F32)
                store_part(z, 0, j, position(z, f), total.astype(BF16))
            start_first(0, j, z)

    def to_dev(p, o):
        dest = lax.rem(me_d + o, n_dev)
        return push(
            blocks.at[dest], gathered.at[me_s, p, me_d],
            a_send.at[p, o], a_recv.at[p, o], (me_s, dest),
        )

    def from_dev(p, o):
        src = lax.rem(me_d + n_dev - o, n_dev)
        return push(
            blocks.at[me_d], gathered.at[me_s, p, src],
            a_send.at[p, o], a_recv.at[p, o], (me_s, src),
        )

    contract = (((1,), (1,)), ((), ()))

    def transform(p):
        @pl.loop(0, n_dev // 2)
        def _(h):
            at = pl.ds(pl.multiple_of(h * 2 * chans, 2 * chans), 2 * chans)
            both = lax.dot_general(
                tables[0, at, :], stack[...], contract, preferred_element_type=F32
            ) + lax.dot_general(
                tables[1, at, :], turned[...], contract, preferred_element_type=F32
            )
            both = both.astype(BF16)
            for e in range(2):
                for z in range(2):
                    blocks[h * 2 + e, z] = both[
                        e * chans : (e + 1) * chans, z * TILES : (z + 1) * TILES
                    ]

        @pl.loop(1, n_dev)
        def _(o):
            to_dev(p, o).start()

        gathered[me_s, p, me_d] = blocks[me_d]

    first = me_d * chans
    n_hi = chans // LOW

    def low_at(i, trig):
        return pl.ds((i * 2 + trig) * TILES, TILES)

    def weights_low():
        d = delays[...].T * (1.0 / channels)
        for h in range(n_beam // TILES):
            cut = d[:, h * TILES : (h + 1) * TILES]
            for i in range(LOW):
                c, s = turn_trig(cut * float(i))
                share[low_at(h * LOW + i, 0), :] = c
                share[low_at(h * LOW + i, 1), :] = s

    def weights(k):
        d = delays[...].T * (1.0 / channels)
        for h in range(n_beam // TILES):
            cut = slice(h * TILES, (h + 1) * TILES)
            ca, sa = turn_trig(d[:, cut] * (first + k * LOW).astype(F32))
            for i in range(LOW):
                cb, sb = share[low_at(h * LOW + i, 0), :], share[low_at(h * LOW + i, 1), :]
                big[k * LOW + i, :TILES, cut] = (ca * cb - sa * sb).astype(BF16)
                big[k * LOW + i, TILES:, cut] = (sa * cb + ca * sb).astype(BF16)

    strip = chans // QUARTERS

    def cut_of(p, q):
        return pl.ds(0, chans) if p else pl.ds(q * strip, strip)

    def unit(p, o, q, s):
        src = lax.rem(me_d + n_dev - o, n_dev)
        return gathered.at[s, p, src, :, cut_of(p, q)]

    def direct_x(p, o, q):
        here = unit(p, o, q, me_s)
        return push(here, here, gx_send.at[p, q, o], gx_recv.at[p, q, o], (across, me_d))

    def direct_y(p, o, q, i):
        here = unit(p, o, q, me_s)
        return push(
            here, here, gy_send.at[p, q, o, i - 1], gy_recv.at[p, q, o, i - 1],
            (at_row(i) * 2 + side, me_d),
        )

    def spread(p, o, q):
        direct_x(p, o, q).start()
        for i in range(1, rows):
            direct_y(p, o, q, i).start()

    def by_row(p, o, q, i):
        block = unit(p, o, q, across)
        return push(
            block, block, ry_send.at[p, q, o, i - 1], ry_recv.at[p, q, o, i - 1],
            (at_row(i) * 2 + side, me_d),
        )

    def by_side(p, o, q, i):
        block = unit(p, o, q, at_row(rows - i) * 2 + side)
        return push(
            block, block, rx_send.at[p, q, o, i - 1], rx_recv.at[p, q, o, i - 1], (across, me_d)
        )

    def relays(p, o, q):
        kind = by_row if o % 2 == 0 else by_side
        return [kind(p, o, q, i) for i in range(1, rows)]

    def relay(p, o, q):
        direct_x(p, o, q).wait_recv()
        for i in range(1, rows):
            direct_y(p, o, q, i).wait_recv()
        for copy in relays(p, o, q):
            copy.start()

    order = [0] + [o for pair in zip(range(1, n_dev), range(n_dev - 1, 0, -1)) for o in pair][: n_dev - 1]
    early = list(range(phases - 1, 0, -1))

    @pl.loop(0, n_chunk)
    def _(j):
        for p in early:
            middle(p, j)
        late_frames(j)

    for p in early:
        @pl.loop(0, n_chunk)
        def _(j):
            finish(p, j)

        transform(p)

    weights_low()
    per = n_hi // n_chunk

    @pl.loop(0, n_chunk)
    def _(j):
        for k in range(per):
            weights(j * per + k)
        middle(0, j)

    for p in early:
        for o in order:
            if o:
                from_dev(p, o).wait_recv()
            spread(p, o, 0)

        @pl.loop(1, n_dev)
        def _(o):
            to_dev(p, o).wait_send()

    @pl.loop(0, n_chunk)
    def _(j):
        finish(0, j)

    transform(0)
    for p in early:
        for o in order:
            relay(p, o, 0)

    units = [(o, q) for q in range(QUARTERS) for o in order]
    for n in range(len(units) + LAG):
        if n < len(units):
            o, q = units[n]
            if o and q == 0:
                from_dev(0, o).wait_recv()
            spread(0, o, q)
        if n >= LAG:
            o, q = units[n - LAG]
            relay(0, o, q)

    @pl.loop(0, n_chunk)
    def _(j):
        for p in range(phases):
            s1x(p, j).wait_send()
            for i in range(1, rows):
                s1y(p, j, i).wait_send()
                s2x(p, j, i).wait_send()
            s2y(p, j).wait_send()
        for z in range(2):
            @pl.when(me_d < n_dev - 1)
            def _():
                history(j, z).wait_send()

    for p in early:
        for o in order:
            for copy in relays(p, o, 0):
                copy.wait_recv()

    over_time = (((0,), (0,)), ((), ()))
    mine = pl.multiple_of(me_s * own, own)
    for q in range(QUARTERS):
        for o in order:
            for copy in relays(0, o, q):
                copy.wait_recv()

        @pl.loop(0, n_dev)
        def _(d):
            for p in range(phases):
                for s in range(n_sect):
                    for z in range(2):
                        line = z * times + d * frames + p * n_sect + s
                        block = gathered[s, p, d, z, q * strip : (q + 1) * strip, :]
                        share[pl.ds(line, strip, stride=2 * times), :] = block.astype(F32)

        @pl.loop(0, strip // 4)
        def _(step):
            for e in range(4):
                i = step * 4 + e
                c = q * strip + i
                both = share[pl.ds(pl.multiple_of(i * 2 * times, 2 * times), 2 * times), :]
                both = both.astype(BF16)
                real, quad = both[:times], both[times:]
                straight = jnp.concatenate([real, quad], axis=1)
                swapped = jnp.concatenate([quad, -real], axis=1)
                lines = jnp.concatenate([straight, swapped], axis=0)
                beam = jnp.dot(lines, big[c], preferred_element_type=F32) * beam_scale
                beams[0, c] = beam[:times].astype(BF16)
                beams[1, c] = beam[times:].astype(BF16)
                left = jnp.concatenate(
                    [both, jnp.concatenate([quad, -real], axis=0)], axis=1
                )
                full[e] = lax.dot_general(left, both, over_time, preferred_element_type=F32)
                vis[0, c] = full[e, pl.ds(mine, own), :] * vis_scale
                vis[1, c] = full[e, pl.ds(pl.multiple_of(mine + TILES, own), own), :] * vis_scale

    for p in range(phases):
        for o in order:
            for q in range(1 if p else QUARTERS):
                direct_x(p, o, q).wait_send()
                for i in range(1, rows):
                    direct_y(p, o, q, i).wait_send()
                for copy in relays(p, o, q):
                    copy.wait_send()

    @pl.loop(1, n_dev)
    def _(o):
        to_dev(0, o).wait_send()


def correlate(voltages, filter_taps, feed_tile, bad_feed, delays, n_sect, n_dev, vis_scale, beam_scale):
    _, feeds, samples = voltages.shape
    channels = filter_taps.shape[1]
    frames = samples // channels
    phases = frames // n_sect
    rows = n_sect // 2
    n_beam = delays.shape[0]
    chans = channels // n_dev
    times = frames * n_dev
    depth = 2 * TILES
    groups = feeds // depth
    width = n_beam
    n_chunk = channels // width
    pieces = TILES // times
    own = TILES // n_sect
    keep = 2 * channels * (TAPS - 1)
    strip = chans // QUARTERS
    shared = max(keep, strip * 2 * times, LOW * 2 * n_beam)
    dma = pltpu.SemaphoreType.DMA
    vmem = pltpu.VMEM
    any_spec = pl.BlockSpec(memory_space=pl.ANY)
    vmem_spec = pl.BlockSpec(memory_space=vmem)
    piece = (times, width)
    return pl.pallas_call(
        functools.partial(correlate_kernel, n_sect, n_dev, vis_scale, beam_scale),
        out_shape=(
            jax.ShapeDtypeStruct((2, chans, own, TILES), F32),
            jax.ShapeDtypeStruct((2, chans, times, n_beam), BF16),
        ),
        in_specs=[any_spec] * 5,
        out_specs=(vmem_spec, vmem_spec),
        scratch_shapes=[
            vmem((max(2 * n_chunk * frames * groups, chans), depth, width), BF16),
            vmem(filter_taps.shape, F32),
            vmem((1, feeds), jnp.int32),
            vmem((1, feeds), jnp.int32),
            vmem(delays.shape, F32),
            vmem((groups, TILES, depth), BF16),
            vmem((max(frames, n_chunk), TILES, width), F32),
            vmem((shared, TILES), F32),
            vmem((2, channels, channels), BF16),
            vmem((2 * TILES, channels), BF16),
            vmem((2 * TILES, channels), BF16),
            vmem((n_dev, 2, chans, TILES), BF16),
            vmem((4, 2 * TILES, TILES), F32),
            vmem((n_sect, phases, n_dev, 2, chans, TILES), BF16),
            vmem((n_chunk, 2, TAPS - 1, TILES, width), BF16),
            vmem((n_chunk, 2, TAPS - 1, TILES, width), BF16),
            vmem((phases, n_chunk, rows * pieces) + piece, BF16),
            vmem((phases, n_chunk, rows - 1, 2 * pieces) + piece, BF16),
            vmem((phases, n_chunk, rows - 1, pieces) + piece, BF16),
            vmem((phases, n_chunk, pieces) + piece, BF16),
            dma((4,)), dma((n_chunk, 2, frames)),
            dma((n_chunk, 2)), dma((n_chunk, 2)),
            dma((phases, n_chunk)), dma((phases, n_chunk)),
            dma((phases, n_chunk, rows - 1)), dma((phases, n_chunk, rows - 1)),
            dma((phases, n_chunk, rows - 1)), dma((phases, n_chunk, rows - 1)),
            dma((phases, n_chunk)), dma((phases, n_chunk)),
            dma((phases, n_dev)), dma((phases, n_dev)),
            dma((phases, QUARTERS, n_dev)), dma((phases, QUARTERS, n_dev)),
            dma((phases, QUARTERS, n_dev, rows - 1)), dma((phases, QUARTERS, n_dev, rows - 1)),
            dma((phases, QUARTERS, n_dev, rows - 1)), dma((phases, QUARTERS, n_dev, rows - 1)),
            dma((phases, QUARTERS, n_dev, rows - 1)), dma((phases, QUARTERS, n_dev, rows - 1)),
        ],
        compiler_params=pltpu.CompilerParams(
            collective_id=0, has_side_effects=True, vmem_limit_bytes=38 * 2**20
        ),
    )(
        voltages.reshape(2, groups, depth, samples), filter_taps,
        feed_tile.reshape(1, feeds), bad_feed.reshape(1, feeds), delays,
    )


def write_kernel(vis_in, beams_in, vis, beams, sems):
    copies = [
        pltpu.make_async_copy(vis_in, vis, sems.at[0]),
        pltpu.make_async_copy(beams_in, beams, sems.at[1]),
    ]
    for copy in copies:
        copy.start()
    for copy in copies:
        copy.wait()


def write(vis, beams):
    vmem_spec = pl.BlockSpec(memory_space=pltpu.VMEM)
    any_spec = pl.BlockSpec(memory_space=pl.ANY)
    return pl.pallas_call(
        write_kernel,
        out_shape=tuple(jax.ShapeDtypeStruct(x.shape, x.dtype) for x in (vis, beams)),
        in_specs=[vmem_spec, vmem_spec],
        out_specs=(any_spec, any_spec),
        scratch_shapes=[pltpu.SemaphoreType.DMA((2,))],
        compiler_params=pltpu.CompilerParams(vmem_limit_bytes=2**20),
    )(vis, beams)


def local(voltages, filter_taps, feed_tile, bad_feed, delays):
    channels = filter_taps.shape[1]
    n_dev = lax.axis_size("dev")
    n_sect = lax.axis_size("sect")
    total_frames = voltages.shape[2] // channels * n_dev
    vis, beams = correlate(
        voltages, filter_taps, feed_tile, bad_feed, delays, n_sect, n_dev,
        1.0 / (total_frames * FEEDS / TILES), 1.0 / math.sqrt(FEEDS),
    )
    vis, beams = write(vis, beams)
    return vis, jnp.transpose(beams, (0, 1, 3, 2))


def solution(mesh):
    return jax.shard_map(
        local,
        mesh=mesh,
        in_specs=(P(None, "sect", "dev"), P(), P("sect"), P("sect"), P("sect", None)),
        out_specs=(P(None, "dev", "sect", None), P(None, "dev", "sect", None)),
        check_vma=False,
    )
```

```python
import functools
import math

import jax
import jax.numpy as jnp
from jax import lax
from jax.experimental import pallas as pl
from jax.experimental.pallas import tpu as pltpu
from jax.sharding import PartitionSpec as P

FEEDS = 2048
TILES = 128
TAPS = 4
PARTS = 2
LAG = 4
GROUP = 16
STEP = 32

MESH = pl.DeviceIdType.MESH
BF16 = jnp.bfloat16
F32 = jnp.float32


def turn_trig(turns):
    r = turns - jnp.round(turns)
    y = r * math.pi
    q = y * y
    s = 0.0
    for n in (11, 9, 7, 5, 3, 1):
        s = s * q + (-1.0) ** ((n - 1) // 2) / math.factorial(n)
    s = s * y
    c = 0.0
    for n in (12, 10, 8, 6, 4, 2, 0):
        c = c * q + (-1.0) ** (n // 2) / math.factorial(n)
    return 1.0 - 2.0 * s * s, 2.0 * s * c


def correlate_kernel(
    n_sect, n_dev, vis_scale, beam_scale,
    volts, taps_in, tile_in, bad_in, delays_in,
    vis, beams,
    big, taps, feed_tile, bad_feed, delays, matrix, sums, kept, tables, stack, turned,
    blocks, lags, ready, gathered, hist_src, hist_land, l1x, l1y, l2x, l2y,
    in_sem, volt_sem, h_send, h_recv, s1x_send, s1x_recv, s1y_send, s1y_recv,
    s2x_send, s2x_recv, s2y_send, s2y_recv, a_send, a_recv,
    gx_send, gx_recv, gy_send, gy_recv, rx_send, rx_recv, ry_send, ry_recv,
):
    me_s, me_d = lax.axis_index("sect"), lax.axis_index("dev")
    rows = n_sect // 2
    side, row = lax.rem(me_s, 2), me_s // 2
    across = row * 2 + 1 - side
    channels = taps.shape[1]
    groups = volts.shape[1]
    frames = volts.shape[3] // channels
    phases = frames // n_sect
    width = big.shape[2]
    n_chunk = channels // width
    _, chans, times, n_beam = beams.shape
    depth = big.shape[1]
    pieces = TILES // times
    own = vis.shape[2]

    def at_row(i):
        return lax.rem(row + i, rows)

    small = [
        pltpu.make_async_copy(a, b, in_sem.at[i])
        for i, (a, b) in enumerate(
            [(tile_in, feed_tile), (bad_in, bad_feed), (taps_in, taps), (delays_in, delays)]
        )
    ]

    def load(j, z, f):
        slot = ((j * 2 + z) * frames + f) * groups
        start = pl.multiple_of(f * channels + j * width, width)
        return pltpu.make_async_copy(
            volts.at[z, :, :, pl.ds(start, width)], big.at[pl.ds(slot, groups)],
            volt_sem.at[j, z, f],
        )

    for copy in small:
        copy.start()

    @pl.loop(0, n_chunk)
    def _(j):
        for z in range(2):
            for f in range(frames):
                load(j, z, f).start()

    barrier = pltpu.get_barrier_semaphore()
    for o in range(1, n_dev):
        pl.semaphore_signal(
            barrier, inc=1, device_id=(me_s, lax.rem(me_d + o, n_dev)), device_id_type=MESH
        )
    pl.semaphore_signal(barrier, inc=1, device_id=(across, me_d), device_id_type=MESH)
    for i in range(1, rows):
        pl.semaphore_signal(
            barrier, inc=1, device_id=(at_row(i) * 2 + side, me_d), device_id_type=MESH
        )

    @pl.when(me_d == 0)
    def _():
        hist_land[...] = jnp.zeros_like(hist_land)

    for copy in small[:2]:
        copy.wait()
    tile_ids = lax.broadcasted_iota(jnp.int32, matrix.shape, 0)
    member = (feed_tile[...] == tile_ids) & (bad_feed[...] == 0)
    matrix[...] = jnp.where(member, 1.0, 0.0).astype(BF16)
    for copy in small[2:]:
        copy.wait()
    pl.semaphore_wait(barrier, n_dev - 1 + rows)

    def push(source, target, send, recv, device):
        return pltpu.make_async_remote_copy(
            src_ref=source, dst_ref=target, send_sem=send, recv_sem=recv,
            device_id=device, device_id_type=MESH,
        )

    def part_at(p, j, pos):
        return ((p * n_chunk + j) * n_sect + pos) * pieces

    def part(z, p, j, pos, count=1):
        return beams.at[z, pl.ds(part_at(p, j, pos), count * pieces)]

    def store_part(z, p, j, pos, value):
        begin = part_at(p, j, pos)
        for n in range(pieces):
            beams[z, begin + n] = value[n * times : (n + 1) * times]

    def s1x(p, j):
        return push(
            part(0, p, j, (1 - side) * rows, rows), l1x.at[p, j],
            s1x_send.at[p, j], s1x_recv.at[p, j], (across, me_d),
        )

    def s1y(p, j, i):
        other = at_row(i)
        return push(
            part(1, p, j, other * 2, 2), l1y.at[p, j, i - 1],
            s1y_send.at[p, j, i - 1], s1y_recv.at[p, j, i - 1], (other * 2 + side, me_d),
        )

    def s2x(p, j, i):
        other = at_row(i)
        return push(
            part(0, p, j, side * rows + other), l2x.at[p, j, i - 1],
            s2x_send.at[p, j, i - 1], s2x_recv.at[p, j, i - 1], (other * 2 + side, me_d),
        )

    def s2y(p, j):
        return push(
            part(1, p, j, row * 2 + 1 - side), l2y.at[p, j],
            s2y_send.at[p, j], s2y_recv.at[p, j], (across, me_d),
        )

    def start_first(p, j, z):
        if z == 0:
            s1x(p, j).start()
        else:
            for i in range(1, rows):
                s1y(p, j, i).start()

    def history(j, z):
        return push(
            hist_src.at[j, z], hist_land.at[j, z], h_send.at[j, z], h_recv.at[j, z],
            (me_s, lax.rem(me_d + 1, n_dev)),
        )

    def position(z, f):
        s = f % n_sect
        return (s % 2) * rows + s // 2 if z == 0 else s

    def tap(m, j):
        return taps[m : m + 1, pl.ds(pl.multiple_of(j * width, width), width)]

    def head(j):
        for z in range(2):
            for f in range(frames):
                load(j, z, f).wait()
            for f in range(frames):
                slot = ((j * 2 + z) * frames + f) * groups
                block = big[pl.ds(slot, groups)].reshape(groups * depth, width)
                total = jnp.dot(matrix[...], block, preferred_element_type=F32)
                sums[f] = total
                late = f - (frames - TAPS + 1)
                if late >= 0:
                    hist_src[j, z, late] = total.astype(BF16)
            for f in range(frames - 1, -1, -1):
                total = 0.0
                for m in range(min(f + 1, TAPS)):
                    total = total + tap(m, j) * sums[f - m]
                if f >= TAPS - 1:
                    store_part(z, f // n_sect, j, position(z, f), total.astype(BF16))
                else:
                    kept[j, z, f] = total
            for p in range(phases - 1, 0, -1):
                start_first(p, j, z)

            @pl.when(me_d < n_dev - 1)
            def _():
                history(j, z).start()

    def fourier():
        span = STEP
        n_cut = channels // width
        col = lax.broadcasted_iota(jnp.int32, (span, channels), 1).astype(F32)
        line = lax.broadcasted_iota(jnp.int32, (span, channels), 0).astype(F32)
        cb, sb = turn_trig(line * col * (1.0 / channels))
        factor = 1.0 / math.sqrt(channels)
        for n in range(n_cut):
            cut = slice(n * width, (n + 1) * width)
            sums[n, :span, :] = cb[:, cut] * factor
            sums[n, span : 2 * span, :] = sb[:, cut] * factor
        one = lax.broadcasted_iota(jnp.int32, (8, width), 1).astype(F32)

        @pl.loop(0, channels // span)
        def _(k):
            for n in range(n_cut):
                turns = (one + float(n * width)) * (k * span).astype(F32) * (1.0 / channels)
                ca, sa = turn_trig(turns)
                ca, sa = ca[:1], sa[:1]
                low_c, low_s = sums[n, :span, :], sums[n, span : 2 * span, :]
                at = pl.ds(pl.multiple_of(k * span, span), span)
                cut = slice(n * width, (n + 1) * width)
                tables[0, at, cut] = (ca * low_c - sa * low_s).astype(BF16)
                tables[1, at, cut] = (sa * low_c + ca * low_s).astype(BF16)

    def add(*terms):
        total = terms[0].astype(F32)
        for term in terms[1:]:
            total = total + term.astype(F32)
        return total.astype(BF16)

    def middle(p, j):
        s1x(p, j).wait_recv()
        for i in range(1, rows):
            other = at_row(i)
            begin = part_at(p, j, side * rows + other)
            for n in range(pieces):
                beams[0, begin + n] = add(beams[0, begin + n], l1x[p, j, other * pieces + n])
            s2x(p, j, i).start()
        for i in range(1, rows):
            s1y(p, j, i).wait_recv()
        begin = part_at(p, j, row * 2 + 1 - side)
        for n in range(pieces):
            beams[1, begin + n] = add(
                beams[1, begin + n],
                *[l1y[p, j, i - 1, (1 - side) * pieces + n] for i in range(1, rows)],
            )
        s2y(p, j).start()

    def finish(p, j):
        at = pl.ds(pl.multiple_of(j * width, width), width)
        for i in range(1, rows):
            s2x(p, j, i).wait_recv()
        begin = part_at(p, j, side * rows + row)
        for n in range(pieces):
            value = add(
                beams[0, begin + n], l1x[p, j, row * pieces + n],
                *[l2x[p, j, i - 1, n] for i in range(1, rows)],
            )
            stack[n * times : (n + 1) * times, at] = value
            turned[TILES + n * times : TILES + (n + 1) * times, at] = -value
        s2y(p, j).wait_recv()
        begin = part_at(p, j, row * 2 + side)
        for n in range(pieces):
            value = add(
                beams[1, begin + n], l2y[p, j, n],
                *[l1y[p, j, i - 1, side * pieces + n] for i in range(1, rows)],
            )
            stack[TILES + n * times : TILES + (n + 1) * times, at] = value
            turned[n * times : (n + 1) * times, at] = value

    def late_frames(j):
        for z in range(2):
            @pl.when(me_d > 0)
            def _():
                history(j, z).wait_recv()

            for f in range(TAPS - 1):
                total = kept[j, z, f]
                for m in range(f + 1, TAPS):
                    total = total + tap(m, j) * hist_land[j, z, f - m + TAPS - 1].astype(F32)
                store_part(z, 0, j, position(z, f), total.astype(BF16))
            start_first(0, j, z)

    def to_dev(p, o):
        dest = lax.rem(me_d + o, n_dev)
        return push(
            blocks.at[dest], gathered.at[me_s, p, me_d],
            a_send.at[p, o], a_recv.at[p, o], (me_s, dest),
        )

    def from_dev(p, o):
        src = lax.rem(me_d + n_dev - o, n_dev)
        return push(
            blocks.at[me_d], gathered.at[me_s, p, src],
            a_send.at[p, o], a_recv.at[p, o], (me_s, src),
        )

    order = [0] + [o for pair in zip(range(1, n_dev), range(n_dev - 1, 0, -1)) for o in pair][: n_dev - 1]
    early = list(range(phases - 1, 0, -1))
    contract = (((1,), (1,)), ((), ()))

    def transform(p):
        @pl.loop(0, n_dev // 2)
        def _(h):
            at = pl.ds(pl.multiple_of(h * 2 * chans, 2 * chans), 2 * chans)
            both = lax.dot_general(
                tables[0, at, :], stack[...], contract, preferred_element_type=F32
            ) + lax.dot_general(
                tables[1, at, :], turned[...], contract, preferred_element_type=F32
            )
            both = both.astype(BF16)
            for e in range(2):
                for z in range(2):
                    blocks[h * 2 + e, z] = both[
                        e * chans : (e + 1) * chans, z * TILES : (z + 1) * TILES
                    ]

        for o in order[1:]:
            to_dev(p, o).start()

        gathered[me_s, p, me_d] = blocks[me_d]

    first = me_d * chans

    def weights(n):
        across_beams = n_beam // TILES
        r, h = n // across_beams, n % across_beams
        at, cut = slice(r * STEP, (r + 1) * STEP), slice(h * TILES, (h + 1) * TILES)
        low = slice(TILES + r * STEP, TILES + (r + 1) * STEP)
        turns = lags[at, cut]
        uc, us = turn_trig(turns)

        def body(k, now):
            c, s = now
            for e in range(4):
                big[k * 4 + e, at, cut] = c.astype(BF16)
                big[k * 4 + e, low, cut] = s.astype(BF16)
                c, s = c * uc - s * us, s * uc + c * us
            return c, s

        lax.fori_loop(0, chans // 4, body, turn_trig(turns * first.astype(F32)))

    strip = chans // PARTS

    def cut_of(p, q):
        return pl.ds(0, chans) if p else pl.ds(q * strip, strip)

    def unit(p, o, q, s):
        src = lax.rem(me_d + n_dev - o, n_dev)
        return gathered.at[s, p, src, :, cut_of(p, q)]

    def direct_x(p, o, q):
        here = unit(p, o, q, me_s)
        return push(here, here, gx_send.at[p, q, o], gx_recv.at[p, q, o], (across, me_d))

    def direct_y(p, o, q, i):
        here = unit(p, o, q, me_s)
        return push(
            here, here, gy_send.at[p, q, o, i - 1], gy_recv.at[p, q, o, i - 1],
            (at_row(i) * 2 + side, me_d),
        )

    def spread(p, o, q):
        direct_x(p, o, q).start()
        for i in range(1, rows):
            direct_y(p, o, q, i).start()

    def by_row(p, o, q, i):
        block = unit(p, o, q, across)
        return push(
            block, block, ry_send.at[p, q, o, i - 1], ry_recv.at[p, q, o, i - 1],
            (at_row(i) * 2 + side, me_d),
        )

    def by_side(p, o, q, i):
        block = unit(p, o, q, at_row(rows - i) * 2 + side)
        return push(
            block, block, rx_send.at[p, q, o, i - 1], rx_recv.at[p, q, o, i - 1], (across, me_d)
        )

    def relays(p, o, q):
        kind = by_row if o % 2 == 0 else by_side
        return [kind(p, o, q, i) for i in range(1, rows)]

    def relay(p, o, q):
        direct_x(p, o, q).wait_recv()
        for i in range(1, rows):
            direct_y(p, o, q, i).wait_recv()
        for copy in relays(p, o, q):
            copy.start()

    mine = me_s * own
    sign = jnp.where(lax.broadcasted_iota(jnp.int32, (own, 2 * times), 1) < times, 1.0, -1.0)

    def consume(base):
        at = pl.ds(pl.multiple_of(base, GROUP), GROUP)
        for z in range(2):
            for d in range(0, n_dev, 2):
                block = jnp.stack(
                    [
                        gathered[f % n_sect, f // n_sect, d + e, z, at, :].astype(F32)
                        for e in range(2) for f in range(frames)
                    ]
                )
                line = z * times + d * frames
                ready[:, line : line + 2 * frames, :] = jnp.swapaxes(block, 0, 1).astype(BF16)
        for i in range(GROUP):
            c = base + i
            both = ready[i]
            real, quad = both[:times], both[times:]
            straight = jnp.concatenate([real, quad], axis=1)
            swapped = jnp.concatenate([quad, -real], axis=1)
            lines = jnp.concatenate([straight, swapped], axis=0)
            beam = jnp.dot(lines, big[c], preferred_element_type=F32) * beam_scale
            beams[0, c] = beam[:times].astype(BF16)
            beams[1, c] = beam[times:].astype(BF16)
            rolled = pltpu.roll(both.astype(F32), lax.rem(TILES - mine, TILES), 1)
            held = rolled[:, :own].T
            crossed = pltpu.roll(held, times, 1) * sign
            left = jnp.concatenate([held, crossed], axis=0).astype(BF16)
            product = jnp.dot(left, both, preferred_element_type=F32) * vis_scale
            vis[0, c] = product[:own]
            vis[1, c] = product[own:]

    @pl.loop(0, n_chunk)
    def _(j):
        head(j)

        @pl.when(j >= 1)
        def _():
            for p in early:
                middle(p, j - 1)

        @pl.when(j >= 2)
        def _():
            late_frames(j - 2)

    for p in early:
        middle(p, n_chunk - 1)
    fourier()
    lags[...] = delays[...].T * (1.0 / channels)

    @pl.loop(n_chunk - 2, n_chunk)
    def _(j):
        late_frames(j)

    for p in early:
        @pl.loop(0, n_chunk)
        def _(j):
            finish(p, j)

        transform(p)

    work = [functools.partial(weights, n) for n in range(TILES // STEP * (n_beam // TILES))]
    for j in range(n_chunk):
        middle(0, j)
        if len(work) > n_chunk:
            work.pop(0)()

    for p in early:
        for o in order:
            if o:
                from_dev(p, o).wait_recv()
            spread(p, o, 0)

        @pl.loop(1, n_dev)
        def _(o):
            to_dev(p, o).wait_send()

    @pl.loop(0, n_chunk)
    def _(j):
        finish(0, j)

    transform(0)
    for p in early:
        for o in order:
            relay(p, o, 0)
            if work:
                work.pop(0)()
    while work:
        work.pop(0)()

    @pl.loop(0, n_chunk)
    def _(j):
        for p in range(phases):
            s1x(p, j).wait_send()
            for i in range(1, rows):
                s1y(p, j, i).wait_send()
                s2x(p, j, i).wait_send()
            s2y(p, j).wait_send()
        for z in range(2):
            @pl.when(me_d < n_dev - 1)
            def _():
                history(j, z).wait_send()

    strips = [(q, g) for q in range(PARTS) for g in range(strip // GROUP)]
    units = [(o, q) for q in range(PARTS) for o in order]
    arrived = set()

    def work_on(q, g):
        if q not in arrived:
            arrived.add(q)
            for p in early if q == 0 else []:
                for o in order:
                    for copy in relays(p, o, 0):
                        copy.wait_recv()
            for o in order:
                for copy in relays(0, o, q):
                    copy.wait_recv()
        consume(q * strip + g * GROUP)

    for n in range(len(units) + LAG):
        if n < len(units):
            o, q = units[n]
            if o and q == 0:
                from_dev(0, o).wait_recv()
            spread(0, o, q)
        if n >= LAG:
            o, q = units[n - LAG]
            relay(0, o, q)
            if q and strips[0][0] < q:
                work_on(*strips.pop(0))
    for q, g in strips:
        work_on(q, g)

    for p in range(phases):
        for o in order:
            for q in range(1 if p else PARTS):
                direct_x(p, o, q).wait_send()
                for i in range(1, rows):
                    direct_y(p, o, q, i).wait_send()
                for copy in relays(p, o, q):
                    copy.wait_send()

    @pl.loop(1, n_dev)
    def _(o):
        to_dev(0, o).wait_send()


def correlate(voltages, filter_taps, feed_tile, bad_feed, delays, n_sect, n_dev, vis_scale, beam_scale):
    _, feeds, samples = voltages.shape
    channels = filter_taps.shape[1]
    frames = samples // channels
    phases = frames // n_sect
    rows = n_sect // 2
    n_beam = delays.shape[0]
    chans = channels // n_dev
    times = frames * n_dev
    depth = 2 * TILES
    groups = feeds // depth
    width = n_beam
    n_chunk = channels // width
    pieces = TILES // times
    own = TILES // n_sect
    dma = pltpu.SemaphoreType.DMA
    vmem = pltpu.VMEM
    any_spec = pl.BlockSpec(memory_space=pl.ANY)
    vmem_spec = pl.BlockSpec(memory_space=vmem)
    piece = (times, width)
    return pl.pallas_call(
        functools.partial(correlate_kernel, n_sect, n_dev, vis_scale, beam_scale),
        out_shape=(
            jax.ShapeDtypeStruct((2, chans, own, TILES), F32),
            jax.ShapeDtypeStruct((2, chans, times, n_beam), BF16),
        ),
        in_specs=[any_spec] * 5,
        out_specs=(vmem_spec, vmem_spec),
        scratch_shapes=[
            vmem((max(2 * n_chunk * frames * groups, chans), depth, width), BF16),
            vmem(filter_taps.shape, F32),
            vmem((1, feeds), jnp.int32),
            vmem((1, feeds), jnp.int32),
            vmem(delays.shape, F32),
            vmem((TILES, feeds), BF16),
            vmem((max(frames, n_chunk), TILES, width), F32),
            vmem((n_chunk, 2, TAPS - 1, TILES, width), F32),
            vmem((2, channels, channels), BF16),
            vmem((2 * TILES, channels), BF16),
            vmem((2 * TILES, channels), BF16),
            vmem((n_dev, 2, chans, TILES), BF16),
            vmem((TILES, n_beam), F32),
            vmem((GROUP, 2 * times, TILES), BF16),
            vmem((n_sect, phases, n_dev, 2, chans, TILES), BF16),
            vmem((n_chunk, 2, TAPS - 1, TILES, width), BF16),
            vmem((n_chunk, 2, TAPS - 1, TILES, width), BF16),
            vmem((phases, n_chunk, rows * pieces) + piece, BF16),
            vmem((phases, n_chunk, rows - 1, 2 * pieces) + piece, BF16),
            vmem((phases, n_chunk, rows - 1, pieces) + piece, BF16),
            vmem((phases, n_chunk, pieces) + piece, BF16),
            dma((4,)), dma((n_chunk, 2, frames)),
            dma((n_chunk, 2)), dma((n_chunk, 2)),
            dma((phases, n_chunk)), dma((phases, n_chunk)),
            dma((phases, n_chunk, rows - 1)), dma((phases, n_chunk, rows - 1)),
            dma((phases, n_chunk, rows - 1)), dma((phases, n_chunk, rows - 1)),
            dma((phases, n_chunk)), dma((phases, n_chunk)),
            dma((phases, n_dev)), dma((phases, n_dev)),
            dma((phases, PARTS, n_dev)), dma((phases, PARTS, n_dev)),
            dma((phases, PARTS, n_dev, rows - 1)), dma((phases, PARTS, n_dev, rows - 1)),
            dma((phases, PARTS, n_dev, rows - 1)), dma((phases, PARTS, n_dev, rows - 1)),
            dma((phases, PARTS, n_dev, rows - 1)), dma((phases, PARTS, n_dev, rows - 1)),
        ],
        compiler_params=pltpu.CompilerParams(
            collective_id=0, has_side_effects=True, vmem_limit_bytes=40 * 2**20
        ),
    )(
        voltages.reshape(2, groups, depth, samples), filter_taps,
        feed_tile.reshape(1, feeds), bad_feed.reshape(1, feeds), delays,
    )


def write_kernel(vis_in, beams_in, vis, beams, sems):
    copies = [
        pltpu.make_async_copy(vis_in, vis, sems.at[0]),
        pltpu.make_async_copy(beams_in, beams, sems.at[1]),
    ]
    for copy in copies:
        copy.start()
    for copy in copies:
        copy.wait()


def write(vis, beams):
    vmem_spec = pl.BlockSpec(memory_space=pltpu.VMEM)
    any_spec = pl.BlockSpec(memory_space=pl.ANY)
    return pl.pallas_call(
        write_kernel,
        out_shape=tuple(jax.ShapeDtypeStruct(x.shape, x.dtype) for x in (vis, beams)),
        in_specs=[vmem_spec, vmem_spec],
        out_specs=(any_spec, any_spec),
        scratch_shapes=[pltpu.SemaphoreType.DMA((2,))],
        compiler_params=pltpu.CompilerParams(vmem_limit_bytes=2**20),
    )(vis, beams)


def local(voltages, filter_taps, feed_tile, bad_feed, delays):
    channels = filter_taps.shape[1]
    n_dev = lax.axis_size("dev")
    n_sect = lax.axis_size("sect")
    total_frames = voltages.shape[2] // channels * n_dev
    vis, beams = correlate(
        voltages, filter_taps, feed_tile, bad_feed, delays, n_sect, n_dev,
        1.0 / (total_frames * FEEDS / TILES), 1.0 / math.sqrt(FEEDS),
    )
    vis, beams = write(vis, beams)
    return vis, jnp.transpose(beams, (0, 1, 3, 2))


def solution(mesh):
    return jax.shard_map(
        local,
        mesh=mesh,
        in_specs=(P(None, "sect", "dev"), P(), P("sect"), P("sect"), P("sect", None)),
        out_specs=(P(None, "dev", "sect", None), P(None, "dev", "sect", None)),
        check_vma=False,
    )
```

```python
import functools
import math

import jax
import jax.numpy as jnp
from jax import lax
from jax.experimental import pallas as pl
from jax.experimental.pallas import tpu as pltpu
from jax.sharding import PartitionSpec as P

FEEDS = 2048
TILES = 128
TAPS = 4
PARTS = 2
LAG = 6
GROUP = 16
STEP = 32

MESH = pl.DeviceIdType.MESH
BF16 = jnp.bfloat16
F32 = jnp.float32


def turn_trig(turns):
    r = turns - jnp.round(turns)
    y = r * math.pi
    q = y * y
    s = 0.0
    for n in (11, 9, 7, 5, 3, 1):
        s = s * q + (-1.0) ** ((n - 1) // 2) / math.factorial(n)
    s = s * y
    c = 0.0
    for n in (12, 10, 8, 6, 4, 2, 0):
        c = c * q + (-1.0) ** (n // 2) / math.factorial(n)
    return 1.0 - 2.0 * s * s, 2.0 * s * c


def correlate_kernel(
    n_sect, n_dev, vis_scale, beam_scale,
    volts, taps_in, tile_in, bad_in, delays_in,
    vis, beams,
    big, taps, feed_tile, bad_feed, delays, matrix, sums, kept, tables, stack, turned,
    blocks, lags, ready, full, gathered, hist_src, hist_land, l1x, l1y, l2x, l2y,
    in_sem, volt_sem, h_send, h_recv, s1x_send, s1x_recv, s1y_send, s1y_recv,
    s2x_send, s2x_recv, s2y_send, s2y_recv, a_send, a_recv,
    gx_send, gx_recv, gy_send, gy_recv, rx_send, rx_recv, ry_send, ry_recv,
):
    me_s, me_d = lax.axis_index("sect"), lax.axis_index("dev")
    rows = n_sect // 2
    side, row = lax.rem(me_s, 2), me_s // 2
    across = row * 2 + 1 - side
    channels = taps.shape[1]
    groups = volts.shape[1]
    frames = volts.shape[3] // channels
    phases = frames // n_sect
    width = big.shape[2]
    n_chunk = channels // width
    _, chans, times, n_beam = beams.shape
    depth = big.shape[1]
    pieces = TILES // times
    own = vis.shape[2]

    def at_row(i):
        return lax.rem(row + i, rows)

    small = [
        pltpu.make_async_copy(a, b, in_sem.at[i])
        for i, (a, b) in enumerate(
            [(tile_in, feed_tile), (bad_in, bad_feed), (taps_in, taps), (delays_in, delays)]
        )
    ]

    def load(j, z, f):
        slot = ((j * 2 + z) * frames + f) * groups
        start = pl.multiple_of(f * channels + j * width, width)
        return pltpu.make_async_copy(
            volts.at[z, :, :, pl.ds(start, width)], big.at[pl.ds(slot, groups)],
            volt_sem.at[j, z, f],
        )

    for copy in small:
        copy.start()

    @pl.loop(0, n_chunk)
    def _(j):
        for z in range(2):
            for f in range(frames):
                load(j, z, f).start()

    barrier = pltpu.get_barrier_semaphore()
    for o in range(1, n_dev):
        pl.semaphore_signal(
            barrier, inc=1, device_id=(me_s, lax.rem(me_d + o, n_dev)), device_id_type=MESH
        )
    pl.semaphore_signal(barrier, inc=1, device_id=(across, me_d), device_id_type=MESH)
    for i in range(1, rows):
        pl.semaphore_signal(
            barrier, inc=1, device_id=(at_row(i) * 2 + side, me_d), device_id_type=MESH
        )

    @pl.when(me_d == 0)
    def _():
        hist_land[...] = jnp.zeros_like(hist_land)

    for copy in small[:2]:
        copy.wait()
    tile_ids = lax.broadcasted_iota(jnp.int32, matrix.shape, 0)
    member = (feed_tile[...] == tile_ids) & (bad_feed[...] == 0)
    matrix[...] = jnp.where(member, 1.0, 0.0).astype(BF16)
    for copy in small[2:]:
        copy.wait()
    pl.semaphore_wait(barrier, n_dev - 1 + rows)

    def push(source, target, send, recv, device):
        return pltpu.make_async_remote_copy(
            src_ref=source, dst_ref=target, send_sem=send, recv_sem=recv,
            device_id=device, device_id_type=MESH,
        )

    def part_at(p, j, pos):
        return ((p * n_chunk + j) * n_sect + pos) * pieces

    def part(z, p, j, pos, count=1):
        return beams.at[z, pl.ds(part_at(p, j, pos), count * pieces)]

    def store_part(z, p, j, pos, value):
        begin = part_at(p, j, pos)
        for n in range(pieces):
            beams[z, begin + n] = value[n * times : (n + 1) * times]

    def s1x(p, j):
        return push(
            part(0, p, j, (1 - side) * rows, rows), l1x.at[p, j],
            s1x_send.at[p, j], s1x_recv.at[p, j], (across, me_d),
        )

    def s1y(p, j, i):
        other = at_row(i)
        return push(
            part(1, p, j, other * 2, 2), l1y.at[p, j, i - 1],
            s1y_send.at[p, j, i - 1], s1y_recv.at[p, j, i - 1], (other * 2 + side, me_d),
        )

    def s2x(p, j, i):
        other = at_row(i)
        return push(
            part(0, p, j, side * rows + other), l2x.at[p, j, i - 1],
            s2x_send.at[p, j, i - 1], s2x_recv.at[p, j, i - 1], (other * 2 + side, me_d),
        )

    def s2y(p, j):
        return push(
            part(1, p, j, row * 2 + 1 - side), l2y.at[p, j],
            s2y_send.at[p, j], s2y_recv.at[p, j], (across, me_d),
        )

    def start_first(p, j, z):
        if z == 0:
            s1x(p, j).start()
        else:
            for i in range(1, rows):
                s1y(p, j, i).start()

    def history(j, z):
        return push(
            hist_src.at[j, z], hist_land.at[j, z], h_send.at[j, z], h_recv.at[j, z],
            (me_s, lax.rem(me_d + 1, n_dev)),
        )

    def position(z, f):
        s = f % n_sect
        return (s % 2) * rows + s // 2 if z == 0 else s

    def tap(m, j):
        return taps[m : m + 1, pl.ds(pl.multiple_of(j * width, width), width)]

    def head(j):
        for z in range(2):
            for f in range(frames):
                load(j, z, f).wait()
            for f in range(frames):
                slot = ((j * 2 + z) * frames + f) * groups
                block = big[pl.ds(slot, groups)].reshape(groups * depth, width)
                total = jnp.dot(matrix[...], block, preferred_element_type=F32)
                sums[f] = total
                late = f - (frames - TAPS + 1)
                if late >= 0:
                    hist_src[j, z, late] = total.astype(BF16)
            for f in range(frames - 1, -1, -1):
                total = 0.0
                for m in range(min(f + 1, TAPS)):
                    total = total + tap(m, j) * sums[f - m]
                if f >= TAPS - 1:
                    store_part(z, f // n_sect, j, position(z, f), total.astype(BF16))
                else:
                    kept[j, z, f] = total
            for p in range(phases - 1, 0, -1):
                start_first(p, j, z)

            @pl.when(me_d < n_dev - 1)
            def _():
                history(j, z).start()

    def fourier():
        span = STEP
        n_cut = channels // width
        col = lax.broadcasted_iota(jnp.int32, (span, channels), 1).astype(F32)
        line = lax.broadcasted_iota(jnp.int32, (span, channels), 0).astype(F32)
        cb, sb = turn_trig(line * col * (1.0 / channels))
        factor = 1.0 / math.sqrt(channels)
        for n in range(n_cut):
            cut = slice(n * width, (n + 1) * width)
            sums[n, :span, :] = cb[:, cut] * factor
            sums[n, span : 2 * span, :] = sb[:, cut] * factor
        one = lax.broadcasted_iota(jnp.int32, (8, width), 1).astype(F32)

        @pl.loop(0, channels // span)
        def _(k):
            for n in range(n_cut):
                turns = (one + float(n * width)) * (k * span).astype(F32) * (1.0 / channels)
                ca, sa = turn_trig(turns)
                ca, sa = ca[:1], sa[:1]
                low_c, low_s = sums[n, :span, :], sums[n, span : 2 * span, :]
                at = pl.ds(pl.multiple_of(k * span, span), span)
                cut = slice(n * width, (n + 1) * width)
                tables[0, at, cut] = (ca * low_c - sa * low_s).astype(BF16)
                tables[1, at, cut] = (sa * low_c + ca * low_s).astype(BF16)

    def add(*terms):
        total = terms[0].astype(F32)
        for term in terms[1:]:
            total = total + term.astype(F32)
        return total.astype(BF16)

    def middle(p, j):
        s1x(p, j).wait_recv()
        for i in range(1, rows):
            other = at_row(i)
            begin = part_at(p, j, side * rows + other)
            for n in range(pieces):
                beams[0, begin + n] = add(beams[0, begin + n], l1x[p, j, other * pieces + n])
            s2x(p, j, i).start()
        for i in range(1, rows):
            s1y(p, j, i).wait_recv()
        begin = part_at(p, j, row * 2 + 1 - side)
        for n in range(pieces):
            beams[1, begin + n] = add(
                beams[1, begin + n],
                *[l1y[p, j, i - 1, (1 - side) * pieces + n] for i in range(1, rows)],
            )
        s2y(p, j).start()

    def finish(p, j):
        at = pl.ds(pl.multiple_of(j * width, width), width)
        for i in range(1, rows):
            s2x(p, j, i).wait_recv()
        begin = part_at(p, j, side * rows + row)
        for n in range(pieces):
            value = add(
                beams[0, begin + n], l1x[p, j, row * pieces + n],
                *[l2x[p, j, i - 1, n] for i in range(1, rows)],
            )
            stack[n * times : (n + 1) * times, at] = value
            turned[TILES + n * times : TILES + (n + 1) * times, at] = -value
        s2y(p, j).wait_recv()
        begin = part_at(p, j, row * 2 + side)
        for n in range(pieces):
            value = add(
                beams[1, begin + n], l2y[p, j, n],
                *[l1y[p, j, i - 1, side * pieces + n] for i in range(1, rows)],
            )
            stack[TILES + n * times : TILES + (n + 1) * times, at] = value
            turned[n * times : (n + 1) * times, at] = value

    def late_frames(j):
        for z in range(2):
            @pl.when(me_d > 0)
            def _():
                history(j, z).wait_recv()

            for f in range(TAPS - 1):
                total = kept[j, z, f]
                for m in range(f + 1, TAPS):
                    total = total + tap(m, j) * hist_land[j, z, f - m + TAPS - 1].astype(F32)
                store_part(z, 0, j, position(z, f), total.astype(BF16))
            start_first(0, j, z)

    def to_dev(p, o):
        dest = lax.rem(me_d + o, n_dev)
        return push(
            blocks.at[dest], gathered.at[me_s, p, me_d],
            a_send.at[p, o], a_recv.at[p, o], (me_s, dest),
        )

    def from_dev(p, o):
        src = lax.rem(me_d + n_dev - o, n_dev)
        return push(
            blocks.at[me_d], gathered.at[me_s, p, src],
            a_send.at[p, o], a_recv.at[p, o], (me_s, src),
        )

    order = [0] + [o for pair in zip(range(1, n_dev), range(n_dev - 1, 0, -1)) for o in pair][: n_dev - 1]
    early = list(range(phases - 1, 0, -1))
    contract = (((1,), (1,)), ((), ()))

    def transform(p):
        @pl.loop(0, n_dev // 2)
        def _(h):
            at = pl.ds(pl.multiple_of(h * 2 * chans, 2 * chans), 2 * chans)
            both = lax.dot_general(
                tables[0, at, :], stack[...], contract, preferred_element_type=F32
            ) + lax.dot_general(
                tables[1, at, :], turned[...], contract, preferred_element_type=F32
            )
            both = both.astype(BF16)
            for e in range(2):
                for z in range(2):
                    blocks[h * 2 + e, z] = both[
                        e * chans : (e + 1) * chans, z * TILES : (z + 1) * TILES
                    ]

        for o in order[1:]:
            to_dev(p, o).start()

        gathered[me_s, p, me_d] = blocks[me_d]

    first = me_d * chans

    def weights(n):
        across_beams = n_beam // TILES
        r, h = n // across_beams, n % across_beams
        at, cut = slice(r * STEP, (r + 1) * STEP), slice(h * TILES, (h + 1) * TILES)
        low = slice(TILES + r * STEP, TILES + (r + 1) * STEP)
        turns = lags[at, cut]
        uc, us = turn_trig(turns)

        def body(k, now):
            c, s = now
            for e in range(4):
                big[k * 4 + e, at, cut] = c.astype(BF16)
                big[k * 4 + e, low, cut] = s.astype(BF16)
                c, s = c * uc - s * us, s * uc + c * us
            return c, s

        lax.fori_loop(0, chans // 4, body, turn_trig(turns * first.astype(F32)))

    strip = chans // PARTS

    def cut_of(p, q):
        return pl.ds(0, chans) if p else pl.ds(q * strip, strip)

    def unit(p, o, q, s):
        src = lax.rem(me_d + n_dev - o, n_dev)
        return gathered.at[s, p, src, :, cut_of(p, q)]

    def direct_x(p, o, q):
        here = unit(p, o, q, me_s)
        return push(here, here, gx_send.at[p, q, o], gx_recv.at[p, q, o], (across, me_d))

    def direct_y(p, o, q, i):
        here = unit(p, o, q, me_s)
        return push(
            here, here, gy_send.at[p, q, o, i - 1], gy_recv.at[p, q, o, i - 1],
            (at_row(i) * 2 + side, me_d),
        )

    def spread(p, o, q):
        direct_x(p, o, q).start()
        for i in range(1, rows):
            direct_y(p, o, q, i).start()

    def by_row(p, o, q, i):
        block = unit(p, o, q, across)
        return push(
            block, block, ry_send.at[p, q, o, i - 1], ry_recv.at[p, q, o, i - 1],
            (at_row(i) * 2 + side, me_d),
        )

    def by_side(p, o, q, i):
        block = unit(p, o, q, at_row(rows - i) * 2 + side)
        return push(
            block, block, rx_send.at[p, q, o, i - 1], rx_recv.at[p, q, o, i - 1], (across, me_d)
        )

    def relays(p, o, q):
        kind = by_row if o % 2 == 0 else by_side
        return [kind(p, o, q, i) for i in range(1, rows)]

    def relay(p, o, q):
        direct_x(p, o, q).wait_recv()
        for i in range(1, rows):
            direct_y(p, o, q, i).wait_recv()
        for copy in relays(p, o, q):
            copy.start()

    over_time = (((0,), (0,)), ((), ()))
    mine = pl.multiple_of(me_s * own, own)

    def consume(base):
        at = pl.ds(pl.multiple_of(base, GROUP), GROUP)
        for z in range(2):
            for d in range(0, n_dev, 2):
                block = jnp.stack(
                    [
                        gathered[f % n_sect, f // n_sect, d + e, z, at, :].astype(F32)
                        for e in range(2) for f in range(frames)
                    ]
                )
                line = z * times + d * frames
                ready[:, line : line + 2 * frames, :] = jnp.swapaxes(block, 0, 1).astype(BF16)
        for i in range(GROUP):
            c = base + i
            both = ready[i]
            real, quad = both[:times], both[times:]
            straight = jnp.concatenate([real, quad], axis=1)
            swapped = jnp.concatenate([quad, -real], axis=1)
            lines = jnp.concatenate([straight, swapped], axis=0)
            beam = jnp.dot(lines, big[c], preferred_element_type=F32) * beam_scale
            beams[0, c] = beam[:times].astype(BF16)
            beams[1, c] = beam[times:].astype(BF16)
            crossed = jnp.concatenate([quad, -real], axis=0)
            for z, left in enumerate((both, crossed)):
                full[i % 4, z] = lax.dot_general(
                    left, both, over_time, preferred_element_type=F32
                )
                vis[z, c] = full[i % 4, z, pl.ds(mine, own), :] * vis_scale

    @pl.loop(0, n_chunk)
    def _(j):
        head(j)

        @pl.when(j >= 1)
        def _():
            for p in early:
                middle(p, j - 1)

        @pl.when(j >= 2)
        def _():
            late_frames(j - 2)

    for p in early:
        middle(p, n_chunk - 1)
    fourier()
    lags[...] = delays[...].T * (1.0 / channels)

    @pl.loop(n_chunk - 2, n_chunk)
    def _(j):
        late_frames(j)

    for p in early:
        @pl.loop(0, n_chunk)
        def _(j):
            finish(p, j)

        transform(p)

    work = [functools.partial(weights, n) for n in range(TILES // STEP * (n_beam // TILES))]
    for j in range(n_chunk):
        middle(0, j)
        if len(work) > n_chunk:
            work.pop(0)()

    for p in early:
        for o in order:
            if o:
                from_dev(p, o).wait_recv()
            spread(p, o, 0)

        @pl.loop(1, n_dev)
        def _(o):
            to_dev(p, o).wait_send()

    @pl.loop(0, n_chunk)
    def _(j):
        finish(0, j)

    transform(0)
    for p in early:
        for o in order:
            relay(p, o, 0)
            if work:
                work.pop(0)()
    while work:
        work.pop(0)()

    @pl.loop(0, n_chunk)
    def _(j):
        for p in range(phases):
            s1x(p, j).wait_send()
            for i in range(1, rows):
                s1y(p, j, i).wait_send()
                s2x(p, j, i).wait_send()
            s2y(p, j).wait_send()
        for z in range(2):
            @pl.when(me_d < n_dev - 1)
            def _():
                history(j, z).wait_send()

    strips = [(q, g) for q in range(PARTS) for g in range(strip // GROUP)]
    units = [(o, q) for q in range(PARTS) for o in order]
    arrived = set()

    def work_on(q, g):
        if q not in arrived:
            arrived.add(q)
            for p in early if q == 0 else []:
                for o in order:
                    for copy in relays(p, o, 0):
                        copy.wait_recv()
            for o in order:
                for copy in relays(0, o, q):
                    copy.wait_recv()
        consume(q * strip + g * GROUP)

    for n in range(len(units) + LAG):
        if n < len(units):
            o, q = units[n]
            if o and q == 0:
                from_dev(0, o).wait_recv()
            spread(0, o, q)
        if n >= LAG:
            o, q = units[n - LAG]
            relay(0, o, q)
            if q and strips[0][0] < q:
                work_on(*strips.pop(0))
    for q, g in strips:
        work_on(q, g)

    for p in range(phases):
        for o in order:
            for q in range(1 if p else PARTS):
                direct_x(p, o, q).wait_send()
                for i in range(1, rows):
                    direct_y(p, o, q, i).wait_send()
                for copy in relays(p, o, q):
                    copy.wait_send()

    @pl.loop(1, n_dev)
    def _(o):
        to_dev(0, o).wait_send()


def correlate(voltages, filter_taps, feed_tile, bad_feed, delays, n_sect, n_dev, vis_scale, beam_scale):
    _, feeds, samples = voltages.shape
    channels = filter_taps.shape[1]
    frames = samples // channels
    phases = frames // n_sect
    rows = n_sect // 2
    n_beam = delays.shape[0]
    chans = channels // n_dev
    times = frames * n_dev
    depth = 2 * TILES
    groups = feeds // depth
    width = n_beam
    n_chunk = channels // width
    pieces = TILES // times
    own = TILES // n_sect
    dma = pltpu.SemaphoreType.DMA
    vmem = pltpu.VMEM
    any_spec = pl.BlockSpec(memory_space=pl.ANY)
    vmem_spec = pl.BlockSpec(memory_space=vmem)
    piece = (times, width)
    return pl.pallas_call(
        functools.partial(correlate_kernel, n_sect, n_dev, vis_scale, beam_scale),
        out_shape=(
            jax.ShapeDtypeStruct((2, chans, own, TILES), F32),
            jax.ShapeDtypeStruct((2, chans, times, n_beam), BF16),
        ),
        in_specs=[any_spec] * 5,
        out_specs=(vmem_spec, vmem_spec),
        scratch_shapes=[
            vmem((max(2 * n_chunk * frames * groups, chans), depth, width), BF16),
            vmem(filter_taps.shape, F32),
            vmem((1, feeds), jnp.int32),
            vmem((1, feeds), jnp.int32),
            vmem(delays.shape, F32),
            vmem((TILES, feeds), BF16),
            vmem((max(frames, n_chunk), TILES, width), F32),
            vmem((n_chunk, 2, TAPS - 1, TILES, width), F32),
            vmem((2, channels, channels), BF16),
            vmem((2 * TILES, channels), BF16),
            vmem((2 * TILES, channels), BF16),
            vmem((n_dev, 2, chans, TILES), BF16),
            vmem((TILES, n_beam), F32),
            vmem((GROUP, 2 * times, TILES), BF16),
            vmem((4, 2, TILES, TILES), F32),
            vmem((n_sect, phases, n_dev, 2, chans, TILES), BF16),
            vmem((n_chunk, 2, TAPS - 1, TILES, width), BF16),
            vmem((n_chunk, 2, TAPS - 1, TILES, width), BF16),
            vmem((phases, n_chunk, rows * pieces) + piece, BF16),
            vmem((phases, n_chunk, rows - 1, 2 * pieces) + piece, BF16),
            vmem((phases, n_chunk, rows - 1, pieces) + piece, BF16),
            vmem((phases, n_chunk, pieces) + piece, BF16),
            dma((4,)), dma((n_chunk, 2, frames)),
            dma((n_chunk, 2)), dma((n_chunk, 2)),
            dma((phases, n_chunk)), dma((phases, n_chunk)),
            dma((phases, n_chunk, rows - 1)), dma((phases, n_chunk, rows - 1)),
            dma((phases, n_chunk, rows - 1)), dma((phases, n_chunk, rows - 1)),
            dma((phases, n_chunk)), dma((phases, n_chunk)),
            dma((phases, n_dev)), dma((phases, n_dev)),
            dma((phases, PARTS, n_dev)), dma((phases, PARTS, n_dev)),
            dma((phases, PARTS, n_dev, rows - 1)), dma((phases, PARTS, n_dev, rows - 1)),
            dma((phases, PARTS, n_dev, rows - 1)), dma((phases, PARTS, n_dev, rows - 1)),
            dma((phases, PARTS, n_dev, rows - 1)), dma((phases, PARTS, n_dev, rows - 1)),
        ],
        compiler_params=pltpu.CompilerParams(
            collective_id=0, has_side_effects=True, vmem_limit_bytes=40 * 2**20
        ),
    )(
        voltages.reshape(2, groups, depth, samples),
        *[
            pltpu.with_memory_space_constraint(x, pltpu.HBM)
            for x in (filter_taps, feed_tile.reshape(1, feeds), bad_feed.reshape(1, feeds), delays)
        ],
    )


def write_kernel(vis_in, beams_in, vis, beams, sems):
    copies = [
        pltpu.make_async_copy(vis_in, vis, sems.at[0]),
        pltpu.make_async_copy(beams_in, beams, sems.at[1]),
    ]
    for copy in copies:
        copy.start()
    for copy in copies:
        copy.wait()


def write(vis, beams):
    vmem_spec = pl.BlockSpec(memory_space=pltpu.VMEM)
    any_spec = pl.BlockSpec(memory_space=pl.ANY)
    return pl.pallas_call(
        write_kernel,
        out_shape=tuple(jax.ShapeDtypeStruct(x.shape, x.dtype) for x in (vis, beams)),
        in_specs=[vmem_spec, vmem_spec],
        out_specs=(any_spec, any_spec),
        scratch_shapes=[pltpu.SemaphoreType.DMA((2,))],
        compiler_params=pltpu.CompilerParams(vmem_limit_bytes=2**20),
    )(vis, beams)


def local(voltages, filter_taps, feed_tile, bad_feed, delays):
    channels = filter_taps.shape[1]
    n_dev = lax.axis_size("dev")
    n_sect = lax.axis_size("sect")
    total_frames = voltages.shape[2] // channels * n_dev
    vis, beams = correlate(
        voltages, filter_taps, feed_tile, bad_feed, delays, n_sect, n_dev,
        1.0 / (total_frames * FEEDS / TILES), 1.0 / math.sqrt(FEEDS),
    )
    vis, beams = write(vis, beams)
    return vis, jnp.transpose(beams, (0, 1, 3, 2))


def solution(mesh):
    return jax.shard_map(
        local,
        mesh=mesh,
        in_specs=(P(None, "sect", "dev"), P(), P("sect"), P("sect"), P("sect", None)),
        out_specs=(P(None, "dev", "sect", None), P(None, "dev", "sect", None)),
        check_vma=False,
    )
```

```python
import functools
import math

import jax
import jax.numpy as jnp
from jax import lax
from jax.experimental import pallas as pl
from jax.experimental.pallas import tpu as pltpu
from jax.sharding import PartitionSpec as P

FEEDS = 2048
TILES = 128
TAPS = 4
PARTS = 1
EIGHTHS = 8
LAG = 6
GROUP = 16
STEP = 32

MESH = pl.DeviceIdType.MESH
BF16 = jnp.bfloat16
F32 = jnp.float32


def turn_trig(turns):
    r = turns - jnp.round(turns)
    y = r * math.pi
    q = y * y
    s = 0.0
    for n in (11, 9, 7, 5, 3, 1):
        s = s * q + (-1.0) ** ((n - 1) // 2) / math.factorial(n)
    s = s * y
    c = 0.0
    for n in (12, 10, 8, 6, 4, 2, 0):
        c = c * q + (-1.0) ** (n // 2) / math.factorial(n)
    return 1.0 - 2.0 * s * s, 2.0 * s * c


def correlate_kernel(
    n_sect, n_dev, vis_scale, beam_scale,
    volts, taps_in, tile_in, bad_in, delays_in,
    vis, beams,
    big, taps, feed_tile, bad_feed, delays, matrix, sums, kept, tables, stack, turned,
    blocks, lags, ready, full, gathered, hist_src, hist_land, l1x, l1y, l2x, l2y,
    in_sem, volt_sem, h_send, h_recv, s1x_send, s1x_recv, s1y_send, s1y_recv,
    s2x_send, s2x_recv, s2y_send, s2y_recv, a_send, a_recv,
    gx_send, gx_recv, gy_send, gy_recv, rx_send, rx_recv, ry_send, ry_recv,
):
    me_s, me_d = lax.axis_index("sect"), lax.axis_index("dev")
    rows = n_sect // 2
    side, row = lax.rem(me_s, 2), me_s // 2
    across = row * 2 + 1 - side
    channels = taps.shape[1]
    groups = volts.shape[1]
    frames = volts.shape[3] // channels
    phases = frames // n_sect
    width = big.shape[2]
    n_chunk = channels // width
    _, chans, times, n_beam = beams.shape
    depth = big.shape[1]
    pieces = TILES // times
    own = vis.shape[2]

    def at_row(i):
        return lax.rem(row + i, rows)

    small = [
        pltpu.make_async_copy(a, b, in_sem.at[i])
        for i, (a, b) in enumerate(
            [(tile_in, feed_tile), (bad_in, bad_feed), (taps_in, taps), (delays_in, delays)]
        )
    ]

    def load(j, z, f):
        slot = ((j * 2 + z) * frames + f) * groups
        start = pl.multiple_of(f * channels + j * width, width)
        return pltpu.make_async_copy(
            volts.at[z, :, :, pl.ds(start, width)], big.at[pl.ds(slot, groups)],
            volt_sem.at[j, z, f],
        )

    for copy in small:
        copy.start()

    @pl.loop(0, n_chunk)
    def _(j):
        for z in range(2):
            for f in range(frames):
                load(j, z, f).start()

    barrier = pltpu.get_barrier_semaphore()
    for o in range(1, n_dev):
        pl.semaphore_signal(
            barrier, inc=1, device_id=(me_s, lax.rem(me_d + o, n_dev)), device_id_type=MESH
        )
    pl.semaphore_signal(barrier, inc=1, device_id=(across, me_d), device_id_type=MESH)
    for i in range(1, rows):
        pl.semaphore_signal(
            barrier, inc=1, device_id=(at_row(i) * 2 + side, me_d), device_id_type=MESH
        )

    @pl.when(me_d == 0)
    def _():
        hist_land[...] = jnp.zeros_like(hist_land)

    for copy in small[:2]:
        copy.wait()
    tile_ids = lax.broadcasted_iota(jnp.int32, matrix.shape, 0)
    member = (feed_tile[...] == tile_ids) & (bad_feed[...] == 0)
    matrix[...] = jnp.where(member, 1.0, 0.0).astype(BF16)
    for copy in small[2:]:
        copy.wait()
    pl.semaphore_wait(barrier, n_dev - 1 + rows)

    def push(source, target, send, recv, device):
        return pltpu.make_async_remote_copy(
            src_ref=source, dst_ref=target, send_sem=send, recv_sem=recv,
            device_id=device, device_id_type=MESH,
        )

    def part_at(p, j, pos):
        return ((p * n_chunk + j) * n_sect + pos) * pieces

    def part(z, p, j, pos, count=1):
        return beams.at[z, pl.ds(part_at(p, j, pos), count * pieces)]

    def store_part(z, p, j, pos, value):
        begin = part_at(p, j, pos)
        for n in range(pieces):
            beams[z, begin + n] = value[n * times : (n + 1) * times]

    def s1x(p, j):
        return push(
            part(0, p, j, (1 - side) * rows, rows), l1x.at[p, j],
            s1x_send.at[p, j], s1x_recv.at[p, j], (across, me_d),
        )

    def s1y(p, j, i):
        other = at_row(i)
        return push(
            part(1, p, j, other * 2, 2), l1y.at[p, j, i - 1],
            s1y_send.at[p, j, i - 1], s1y_recv.at[p, j, i - 1], (other * 2 + side, me_d),
        )

    def s2x(p, j, i):
        other = at_row(i)
        return push(
            part(0, p, j, side * rows + other), l2x.at[p, j, i - 1],
            s2x_send.at[p, j, i - 1], s2x_recv.at[p, j, i - 1], (other * 2 + side, me_d),
        )

    def s2y(p, j):
        return push(
            part(1, p, j, row * 2 + 1 - side), l2y.at[p, j],
            s2y_send.at[p, j], s2y_recv.at[p, j], (across, me_d),
        )

    def start_first(p, j, z):
        if z == 0:
            s1x(p, j).start()
        else:
            for i in range(1, rows):
                s1y(p, j, i).start()

    def history(j, z):
        return push(
            hist_src.at[j, z], hist_land.at[j, z], h_send.at[j, z], h_recv.at[j, z],
            (me_s, lax.rem(me_d + 1, n_dev)),
        )

    def position(z, f):
        s = f % n_sect
        return (s % 2) * rows + s // 2 if z == 0 else s

    def tap(m, j):
        return taps[m : m + 1, pl.ds(pl.multiple_of(j * width, width), width)]

    def head(j):
        for z in range(2):
            for f in range(frames):
                load(j, z, f).wait()
            for f in range(frames):
                slot = ((j * 2 + z) * frames + f) * groups
                block = big[pl.ds(slot, groups)].reshape(groups * depth, width)
                total = jnp.dot(matrix[...], block, preferred_element_type=F32)
                sums[f] = total
                late = f - (frames - TAPS + 1)
                if late >= 0:
                    hist_src[j, z, late] = total.astype(BF16)
            for f in range(frames - 1, -1, -1):
                total = 0.0
                for m in range(min(f + 1, TAPS)):
                    total = total + tap(m, j) * sums[f - m]
                if f >= TAPS - 1:
                    store_part(z, f // n_sect, j, position(z, f), total.astype(BF16))
                else:
                    kept[j, z, f] = total
            for p in range(phases - 1, 0, -1):
                start_first(p, j, z)

            @pl.when(me_d < n_dev - 1)
            def _():
                history(j, z).start()

    def fourier():
        span = STEP
        n_cut = channels // width
        col = lax.broadcasted_iota(jnp.int32, (span, channels), 1).astype(F32)
        line = lax.broadcasted_iota(jnp.int32, (span, channels), 0).astype(F32)
        cb, sb = turn_trig(line * col * (1.0 / channels))
        factor = 1.0 / math.sqrt(channels)
        for n in range(n_cut):
            cut = slice(n * width, (n + 1) * width)
            sums[n, :span, :] = cb[:, cut] * factor
            sums[n, span : 2 * span, :] = sb[:, cut] * factor
        one = lax.broadcasted_iota(jnp.int32, (8, width), 1).astype(F32)

        @pl.loop(0, channels // span)
        def _(k):
            for n in range(n_cut):
                turns = (one + float(n * width)) * (k * span).astype(F32) * (1.0 / channels)
                ca, sa = turn_trig(turns)
                ca, sa = ca[:1], sa[:1]
                low_c, low_s = sums[n, :span, :], sums[n, span : 2 * span, :]
                at = pl.ds(pl.multiple_of(k * span, span), span)
                cut = slice(n * width, (n + 1) * width)
                tables[0, at, cut] = (ca * low_c - sa * low_s).astype(BF16)
                tables[1, at, cut] = (sa * low_c + ca * low_s).astype(BF16)

    def add(*terms):
        total = terms[0].astype(F32)
        for term in terms[1:]:
            total = total + term.astype(F32)
        return total.astype(BF16)

    def middle(p, j):
        s1x(p, j).wait_recv()
        for i in range(1, rows):
            other = at_row(i)
            begin = part_at(p, j, side * rows + other)
            for n in range(pieces):
                beams[0, begin + n] = add(beams[0, begin + n], l1x[p, j, other * pieces + n])
            s2x(p, j, i).start()
        for i in range(1, rows):
            s1y(p, j, i).wait_recv()
        begin = part_at(p, j, row * 2 + 1 - side)
        for n in range(pieces):
            beams[1, begin + n] = add(
                beams[1, begin + n],
                *[l1y[p, j, i - 1, (1 - side) * pieces + n] for i in range(1, rows)],
            )
        s2y(p, j).start()

    def finish(p, j):
        at = pl.ds(pl.multiple_of(j * width, width), width)
        for i in range(1, rows):
            s2x(p, j, i).wait_recv()
        begin = part_at(p, j, side * rows + row)
        for n in range(pieces):
            value = add(
                beams[0, begin + n], l1x[p, j, row * pieces + n],
                *[l2x[p, j, i - 1, n] for i in range(1, rows)],
            )
            stack[n * times : (n + 1) * times, at] = value
            turned[TILES + n * times : TILES + (n + 1) * times, at] = -value
        s2y(p, j).wait_recv()
        begin = part_at(p, j, row * 2 + side)
        for n in range(pieces):
            value = add(
                beams[1, begin + n], l2y[p, j, n],
                *[l1y[p, j, i - 1, side * pieces + n] for i in range(1, rows)],
            )
            stack[TILES + n * times : TILES + (n + 1) * times, at] = value
            turned[n * times : (n + 1) * times, at] = value

    def late_frames(j):
        for z in range(2):
            @pl.when(me_d > 0)
            def _():
                history(j, z).wait_recv()

            for f in range(TAPS - 1):
                total = kept[j, z, f]
                for m in range(f + 1, TAPS):
                    total = total + tap(m, j) * hist_land[j, z, f - m + TAPS - 1].astype(F32)
                store_part(z, 0, j, position(z, f), total.astype(BF16))
            start_first(0, j, z)

    def to_dev(p, o):
        dest = lax.rem(me_d + o, n_dev)
        return push(
            blocks.at[dest], gathered.at[me_s, p, me_d],
            a_send.at[p, o], a_recv.at[p, o], (me_s, dest),
        )

    def from_dev(p, o):
        src = lax.rem(me_d + n_dev - o, n_dev)
        return push(
            blocks.at[me_d], gathered.at[me_s, p, src],
            a_send.at[p, o], a_recv.at[p, o], (me_s, src),
        )

    order = [0] + [o for pair in zip(range(1, n_dev), range(n_dev - 1, 0, -1)) for o in pair][: n_dev - 1]
    early = list(range(phases - 1, 0, -1))
    contract = (((1,), (1,)), ((), ()))

    def transform(p):
        @pl.loop(0, n_dev // 2)
        def _(h):
            at = pl.ds(pl.multiple_of(h * 2 * chans, 2 * chans), 2 * chans)
            both = lax.dot_general(
                tables[0, at, :], stack[...], contract, preferred_element_type=F32
            ) + lax.dot_general(
                tables[1, at, :], turned[...], contract, preferred_element_type=F32
            )
            both = both.astype(BF16)
            for e in range(2):
                for z in range(2):
                    blocks[h * 2 + e, z] = both[
                        e * chans : (e + 1) * chans, z * TILES : (z + 1) * TILES
                    ]

        for o in order[1:]:
            to_dev(p, o).start()

        gathered[me_s, p, me_d] = blocks[me_d]

    first = me_d * chans

    def weights(n):
        across_beams = n_beam // TILES
        r, h = n // across_beams, n % across_beams
        at, cut = slice(r * STEP, (r + 1) * STEP), slice(h * TILES, (h + 1) * TILES)
        low = slice(TILES + r * STEP, TILES + (r + 1) * STEP)
        turns = lags[at, cut]
        uc, us = turn_trig(turns)

        def body(k, now):
            c, s = now
            for e in range(4):
                big[k * 4 + e, at, cut] = c.astype(BF16)
                big[k * 4 + e, low, cut] = s.astype(BF16)
                c, s = c * uc - s * us, s * uc + c * us
            return c, s

        lax.fori_loop(0, chans // 4, body, turn_trig(turns * first.astype(F32)))

    bounds = [0, chans * EIGHTHS // 8, chans]

    def cut_of(p, q):
        return pl.ds(0, chans) if p else pl.ds(bounds[q], bounds[q + 1] - bounds[q])

    def unit(p, o, q, s):
        src = lax.rem(me_d + n_dev - o, n_dev)
        return gathered.at[s, p, src, :, cut_of(p, q)]

    def direct_x(p, o, q):
        here = unit(p, o, q, me_s)
        return push(here, here, gx_send.at[p, q, o], gx_recv.at[p, q, o], (across, me_d))

    def direct_y(p, o, q, i):
        here = unit(p, o, q, me_s)
        return push(
            here, here, gy_send.at[p, q, o, i - 1], gy_recv.at[p, q, o, i - 1],
            (at_row(i) * 2 + side, me_d),
        )

    def spread(p, o, q):
        direct_x(p, o, q).start()
        for i in range(1, rows):
            direct_y(p, o, q, i).start()

    def by_row(p, o, q, i):
        block = unit(p, o, q, across)
        return push(
            block, block, ry_send.at[p, q, o, i - 1], ry_recv.at[p, q, o, i - 1],
            (at_row(i) * 2 + side, me_d),
        )

    def by_side(p, o, q, i):
        block = unit(p, o, q, at_row(rows - i) * 2 + side)
        return push(
            block, block, rx_send.at[p, q, o, i - 1], rx_recv.at[p, q, o, i - 1], (across, me_d)
        )

    def relays(p, o, q):
        kind = by_row if o % 2 == 0 else by_side
        return [kind(p, o, q, i) for i in range(1, rows)]

    def relay(p, o, q):
        direct_x(p, o, q).wait_recv()
        for i in range(1, rows):
            direct_y(p, o, q, i).wait_recv()
        for copy in relays(p, o, q):
            copy.start()

    over_time = (((0,), (0,)), ((), ()))
    mine = pl.multiple_of(me_s * own, own)

    def consume(base):
        at = pl.ds(pl.multiple_of(base, GROUP), GROUP)
        for z in range(2):
            for d in range(0, n_dev, 2):
                block = jnp.stack(
                    [
                        gathered[f % n_sect, f // n_sect, d + e, z, at, :].astype(F32)
                        for e in range(2) for f in range(frames)
                    ]
                )
                line = z * times + d * frames
                ready[:, line : line + 2 * frames, :] = jnp.swapaxes(block, 0, 1).astype(BF16)
        for i in range(GROUP):
            c = base + i
            both = ready[i]
            real, quad = both[:times], both[times:]
            straight = jnp.concatenate([real, quad], axis=1)
            swapped = jnp.concatenate([quad, -real], axis=1)
            lines = jnp.concatenate([straight, swapped], axis=0)
            beam = jnp.dot(lines, big[c], preferred_element_type=F32) * beam_scale
            beams[0, c] = beam[:times].astype(BF16)
            beams[1, c] = beam[times:].astype(BF16)
            crossed = jnp.concatenate([quad, -real], axis=0)
            for z, left in enumerate((both, crossed)):
                full[i % 4, z] = lax.dot_general(
                    left, both, over_time, preferred_element_type=F32
                )
                vis[z, c] = full[i % 4, z, pl.ds(mine, own), :] * vis_scale

    @pl.loop(0, n_chunk)
    def _(j):
        head(j)

        @pl.when(j >= 1)
        def _():
            for p in early:
                middle(p, j - 1)

        @pl.when(j >= 2)
        def _():
            late_frames(j - 2)

    for p in early:
        middle(p, n_chunk - 1)
    fourier()
    lags[...] = delays[...].T * (1.0 / channels)

    @pl.loop(n_chunk - 2, n_chunk)
    def _(j):
        late_frames(j)

    for p in early:
        @pl.loop(0, n_chunk)
        def _(j):
            finish(p, j)

        transform(p)

    work = [functools.partial(weights, n) for n in range(TILES // STEP * (n_beam // TILES))]
    for j in range(n_chunk):
        middle(0, j)
        if len(work) > n_chunk:
            work.pop(0)()

    for p in early:
        for o in order:
            if o:
                from_dev(p, o).wait_recv()
            spread(p, o, 0)

        @pl.loop(1, n_dev)
        def _(o):
            to_dev(p, o).wait_send()

    @pl.loop(0, n_chunk)
    def _(j):
        finish(0, j)

    transform(0)
    for p in early:
        for o in order:
            relay(p, o, 0)
            if work:
                work.pop(0)()
    while work:
        work.pop(0)()

    @pl.loop(0, n_chunk)
    def _(j):
        for p in range(phases):
            s1x(p, j).wait_send()
            for i in range(1, rows):
                s1y(p, j, i).wait_send()
                s2x(p, j, i).wait_send()
            s2y(p, j).wait_send()
        for z in range(2):
            @pl.when(me_d < n_dev - 1)
            def _():
                history(j, z).wait_send()

    strips = [(q, base) for q in range(PARTS) for base in range(bounds[q], bounds[q + 1], GROUP)]
    units = [(o, q) for q in range(PARTS) for o in order]
    arrived = set()

    def work_on(q, base):
        if q not in arrived:
            arrived.add(q)
            for p in early if q == 0 else []:
                for o in order:
                    for copy in relays(p, o, 0):
                        copy.wait_recv()
            for o in order:
                for copy in relays(0, o, q):
                    copy.wait_recv()
        consume(base)

    for n in range(len(units) + LAG):
        if n < len(units):
            o, q = units[n]
            if o and q == 0:
                from_dev(0, o).wait_recv()
            spread(0, o, q)
        if n >= LAG:
            o, q = units[n - LAG]
            relay(0, o, q)
            if q and strips[0][0] < q:
                work_on(*strips.pop(0))
    for q, base in strips:
        work_on(q, base)

    for p in range(phases):
        for o in order:
            for q in range(1 if p else PARTS):
                direct_x(p, o, q).wait_send()
                for i in range(1, rows):
                    direct_y(p, o, q, i).wait_send()
                for copy in relays(p, o, q):
                    copy.wait_send()

    @pl.loop(1, n_dev)
    def _(o):
        to_dev(0, o).wait_send()


def correlate(voltages, filter_taps, feed_tile, bad_feed, delays, n_sect, n_dev, vis_scale, beam_scale):
    _, feeds, samples = voltages.shape
    channels = filter_taps.shape[1]
    frames = samples // channels
    phases = frames // n_sect
    rows = n_sect // 2
    n_beam = delays.shape[0]
    chans = channels // n_dev
    times = frames * n_dev
    depth = 2 * TILES
    groups = feeds // depth
    width = n_beam
    n_chunk = channels // width
    pieces = TILES // times
    own = TILES // n_sect
    dma = pltpu.SemaphoreType.DMA
    vmem = pltpu.VMEM
    any_spec = pl.BlockSpec(memory_space=pl.ANY)
    vmem_spec = pl.BlockSpec(memory_space=vmem)
    piece = (times, width)
    return pl.pallas_call(
        functools.partial(correlate_kernel, n_sect, n_dev, vis_scale, beam_scale),
        out_shape=(
            jax.ShapeDtypeStruct((2, chans, own, TILES), F32),
            jax.ShapeDtypeStruct((2, chans, times, n_beam), BF16),
        ),
        in_specs=[any_spec] * 5,
        out_specs=(vmem_spec, vmem_spec),
        scratch_shapes=[
            vmem((max(2 * n_chunk * frames * groups, chans), depth, width), BF16),
            vmem(filter_taps.shape, F32),
            vmem((1, feeds), jnp.int32),
            vmem((1, feeds), jnp.int32),
            vmem(delays.shape, F32),
            vmem((TILES, feeds), BF16),
            vmem((max(frames, n_chunk), TILES, width), F32),
            vmem((n_chunk, 2, TAPS - 1, TILES, width), F32),
            vmem((2, channels, channels), BF16),
            vmem((2 * TILES, channels), BF16),
            vmem((2 * TILES, channels), BF16),
            vmem((n_dev, 2, chans, TILES), BF16),
            vmem((TILES, n_beam), F32),
            vmem((GROUP, 2 * times, TILES), BF16),
            vmem((4, 2, TILES, TILES), F32),
            vmem((n_sect, phases, n_dev, 2, chans, TILES), BF16),
            vmem((n_chunk, 2, TAPS - 1, TILES, width), BF16),
            vmem((n_chunk, 2, TAPS - 1, TILES, width), BF16),
            vmem((phases, n_chunk, rows * pieces) + piece, BF16),
            vmem((phases, n_chunk, rows - 1, 2 * pieces) + piece, BF16),
            vmem((phases, n_chunk, rows - 1, pieces) + piece, BF16),
            vmem((phases, n_chunk, pieces) + piece, BF16),
            dma((4,)), dma((n_chunk, 2, frames)),
            dma((n_chunk, 2)), dma((n_chunk, 2)),
            dma((phases, n_chunk)), dma((phases, n_chunk)),
            dma((phases, n_chunk, rows - 1)), dma((phases, n_chunk, rows - 1)),
            dma((phases, n_chunk, rows - 1)), dma((phases, n_chunk, rows - 1)),
            dma((phases, n_chunk)), dma((phases, n_chunk)),
            dma((phases, n_dev)), dma((phases, n_dev)),
            dma((phases, PARTS, n_dev)), dma((phases, PARTS, n_dev)),
            dma((phases, PARTS, n_dev, rows - 1)), dma((phases, PARTS, n_dev, rows - 1)),
            dma((phases, PARTS, n_dev, rows - 1)), dma((phases, PARTS, n_dev, rows - 1)),
            dma((phases, PARTS, n_dev, rows - 1)), dma((phases, PARTS, n_dev, rows - 1)),
        ],
        compiler_params=pltpu.CompilerParams(
            collective_id=0, has_side_effects=True, vmem_limit_bytes=40 * 2**20
        ),
    )(
        voltages.reshape(2, groups, depth, samples),
        *[
            pltpu.with_memory_space_constraint(x, pltpu.HBM)
            for x in (filter_taps, feed_tile.reshape(1, feeds), bad_feed.reshape(1, feeds), delays)
        ],
    )


def write_kernel(vis_in, beams_in, vis, beams, sems):
    copies = [
        pltpu.make_async_copy(vis_in, vis, sems.at[0]),
        pltpu.make_async_copy(beams_in, beams, sems.at[1]),
    ]
    for copy in copies:
        copy.start()
    for copy in copies:
        copy.wait()


def write(vis, beams):
    vmem_spec = pl.BlockSpec(memory_space=pltpu.VMEM)
    any_spec = pl.BlockSpec(memory_space=pl.ANY)
    return pl.pallas_call(
        write_kernel,
        out_shape=tuple(jax.ShapeDtypeStruct(x.shape, x.dtype) for x in (vis, beams)),
        in_specs=[vmem_spec, vmem_spec],
        out_specs=(any_spec, any_spec),
        scratch_shapes=[pltpu.SemaphoreType.DMA((2,))],
        compiler_params=pltpu.CompilerParams(vmem_limit_bytes=2**20),
    )(vis, beams)


def local(voltages, filter_taps, feed_tile, bad_feed, delays):
    channels = filter_taps.shape[1]
    n_dev = lax.axis_size("dev")
    n_sect = lax.axis_size("sect")
    total_frames = voltages.shape[2] // channels * n_dev
    vis, beams = correlate(
        voltages, filter_taps, feed_tile, bad_feed, delays, n_sect, n_dev,
        1.0 / (total_frames * FEEDS / TILES), 1.0 / math.sqrt(FEEDS),
    )
    vis, beams = write(vis, beams)
    return vis, jnp.transpose(beams, (0, 1, 3, 2))


def solution(mesh):
    return jax.shard_map(
        local,
        mesh=mesh,
        in_specs=(P(None, "sect", "dev"), P(), P("sect"), P("sect"), P("sect", None)),
        out_specs=(P(None, "dev", "sect", None), P(None, "dev", "sect", None)),
        check_vma=False,
    )
```
